256 devices in a mesh: gx: 8 (over x, core), gy: 8 (over z), cyc: 4 (over y).
Axes of the slice: x: 4, y: 4, z: 8, core: 2. Of those that a mesh axis runs over, the one named last changes fastest.
Arguments:
- displacement: bfloat16 [2, 192, 1024, 1024], P(None, 'gx', 'gy', 'cyc'), may hold values from -6 to 6
Outputs:
- basis: float32 [2, 192, 1024, 128], P(None, 'gx', 'gy', 'cyc')
The draws below stay inside these ranges and needn't reach their ends.
All inputs are finite; a program needn't handle non-finite values.
Results may differ from the reference program's by a relative error of at most 0.0003.
Values may be sent and summed in bfloat16 or wider, within the bound.
No kernel may reach another device: no remote copies, remote signals or barrier semaphores. Data moves between devices by JAX's collectives and lax.ppermute only.
A program may use at most 128 MiB of HBM per device.

```python
import jax
import jax.numpy as jnp
from jax import lax

SNAP_DEV = 256
RANK = 128
POWER = 3
NX = 192
NY = 1024
SNAPS = 1024
N_CYC = 4


def steps_of(own_key, extent, cuts, low, high):
    level = 1.0
    for position, shards_of in cuts:
        heights = jax.random.uniform(jax.random.fold_in(jax.random.fold_in(own_key, 6), position), (shards_of,), jnp.float32, low / len(cuts), high / len(cuts))
        level = level * jnp.repeat(jnp.exp(heights), extent[position] // shards_of).reshape((-1,) + (1,) * (len(extent) - 1 - position))
    return level


def noise(stream_key, dims, scale, bound, shards=(), held_as=jnp.bfloat16):
    array = scale * jax.random.normal(stream_key, dims, jnp.float32)
    if shards:
        array = array * steps_of(stream_key, dims, shards, -0.22, 0.18)
    return jnp.clip(array, -bound, bound).astype(held_as)


def setup_inputs(seed: int = 0) -> dict:
    arg_keys = jax.random.split(jax.random.key(seed), 2)
    displacement = noise(arg_keys[0], (2, NX, NY, SNAPS), 1.0, 6.0, ((1, 8), (2, 8), (3, 4)))
    return dict(displacement=displacement)


def strain_rows(padded):
    field = padded.astype(jnp.float32)
    along_x = (field[:, 2:, 1:-1] - field[:, :-2, 1:-1]) * 0.5
    along_y = (field[:, 1:-1, 2:] - field[:, 1:-1, :-2]) * 0.5
    strain_xx = along_x[0]
    strain_yy = along_y[1]
    strain_xy = 0.5 * (along_x[1] + along_y[0])
    first = strain_xx + strain_yy
    second = strain_xx * strain_yy - strain_xy * strain_xy
    return jnp.stack([first, second]).reshape(-1, padded.shape[-1])

def gram_of(joined):
    return lax.dot_general(joined.astype(jnp.float32), joined.astype(jnp.float32), (((0,), (0,)), ((), ())), precision=lax.Precision.HIGHEST, preferred_element_type=jnp.float32)

def finish(joined, gram):
    width = gram.shape[0]
    normed = gram / (jnp.trace(gram) / width + 1e-06)
    vectors = (jnp.arange(width)[:, None] % RANK == jnp.arange(RANK)[None, :]).astype(jnp.float32)
    for step in range(POWER):
        moved = jnp.dot(normed.astype(jnp.float32), vectors.astype(jnp.float32), precision=lax.Precision.HIGHEST, preferred_element_type=jnp.float32)
        lower = jnp.linalg.cholesky(gram_of(moved))
        vectors = lax.linalg.triangular_solve(lower, moved, left_side=False, lower=True, transpose_a=True)
    return jnp.dot(joined.astype(jnp.float32), vectors.astype(jnp.float32), precision=lax.Precision.HIGHEST, preferred_element_type=jnp.float32)

def truncate(joined):
    return finish(joined, gram_of(joined))

def reference(displacement):
    pieces = []
    for group in range(N_CYC):
        block = displacement[..., group * SNAP_DEV:(group + 1) * SNAP_DEV]
        padded = jnp.pad(block, ((0, 0), (1, 1), (1, 1), (0, 0)))
        pieces.append(truncate(strain_rows(padded)))
    pair_low = truncate(jnp.concatenate([pieces[0], pieces[1]], axis=1))
    pair_high = truncate(jnp.concatenate([pieces[2], pieces[3]], axis=1))
    basis = truncate(jnp.concatenate([pair_low, pair_high], axis=1))
    return basis.reshape(2, NX, NY, RANK)
```

```python
import jax
import jax.numpy as jnp
from jax import lax
from jax.sharding import PartitionSpec as P

RANK = 128
POWER = 3


def edges(block, axis, dim):
    count = lax.axis_size(axis)
    forward = [(i, i + 1) for i in range(count - 1)]
    backward = [(target, source) for source, target in forward]
    low = lax.ppermute(
        lax.slice_in_dim(block, block.shape[dim] - 1, None, axis=dim), axis, forward
    )
    high = lax.ppermute(lax.slice_in_dim(block, 0, 1, axis=dim), axis, backward)
    return low, high


def swapped(value, axis, stride):
    mask = 2**stride
    pairs = [(source, source ^ mask) for source in range(lax.axis_size(axis))]
    return lax.ppermute(value, axis, pairs)


def scatter_sum(value, axis):
    count = lax.axis_size(axis)
    parts = lax.all_to_all(value, axis, 0, 0, tiled=True)
    return parts.reshape(count, -1, value.shape[1]).sum(0)


def gathered(value, axis):
    count = lax.axis_size(axis)
    copies = jnp.broadcast_to(value[None], (count,) + value.shape)
    return lax.all_to_all(copies.reshape(-1, value.shape[1]), axis, 0, 0, tiled=True)


def all_sum(value):
    flat = value.reshape(-1, 128)
    part = scatter_sum(flat, "gx")
    part = gathered(part, "gy").reshape(lax.axis_size("gy"), -1, 128).sum(0)
    return gathered(part, "gx").reshape(value.shape)


def strain_rows(block):
    x_low, x_high = edges(block, "gx", 1)
    y_low, y_high = edges(block, "gy", 2)
    field = block.astype(jnp.float32)
    x_pad = jnp.concatenate([x_low, block, x_high], axis=1).astype(jnp.float32)
    y_pad = jnp.concatenate([y_low, block, y_high], axis=2).astype(jnp.float32)
    along_x = (x_pad[:, 2:] - x_pad[:, :-2]) * 0.5
    along_y = (y_pad[:, :, 2:] - y_pad[:, :, :-2]) * 0.5
    strain_xx = along_x[0]
    strain_yy = along_y[1]
    strain_xy = 0.5 * (along_x[1] + along_y[0])
    first = strain_xx + strain_yy
    second = strain_xx * strain_yy - strain_xy * strain_xy
    return jnp.stack([first, second]).reshape(-1, field.shape[-1])


def gram_of(joined):
    return lax.dot_general(
        joined,
        joined,
        (((0,), (0,)), ((), ())),
        precision=lax.Precision.HIGHEST,
        preferred_element_type=jnp.float32,
    )


def matmul_high(left, right):
    return jnp.dot(left, right, precision=lax.Precision.HIGHEST, preferred_element_type=jnp.float32)


def vectors_of(gram):
    width = gram.shape[0]
    normed = gram / (jnp.trace(gram) / width + 1e-06)
    vectors = (jnp.arange(width)[:, None] % RANK == jnp.arange(RANK)[None, :]).astype(jnp.float32)
    for step in range(POWER):
        moved = matmul_high(normed, vectors)
        lower = jnp.linalg.cholesky(gram_of(moved))
        vectors = lax.linalg.triangular_solve(
            lower, moved, left_side=False, lower=True, transpose_a=True
        )
    return vectors


def finish(joined, gram):
    return matmul_high(joined, vectors_of(gram))


def truncate(joined):
    return finish(joined, all_sum(gram_of(joined)))


def own_columns(whole):
    groups = lax.axis_size("cyc")
    share = whole.shape[1] // groups
    return lax.dynamic_slice_in_dim(whole, lax.axis_index("cyc") * share, share, 1)


def on_device(displacement):
    local_rows = displacement.shape[1]
    local_cols = displacement.shape[2]
    piece = truncate(strain_rows(displacement))
    group = lax.axis_index("cyc")
    for level in range(lax.axis_size("cyc").bit_length() - 1):
        partner = swapped(piece, "cyc", level)
        is_low = group >> level & 1 == 0
        first_half = jnp.where(is_low, piece, partner)
        second_half = jnp.where(is_low, partner, piece)
        piece = truncate(jnp.concatenate([first_half, second_half], axis=1))
    result = own_columns(piece)
    return result.reshape(2, local_rows, local_cols, result.shape[1])


def solution(mesh):
    return jax.shard_map(
        on_device,
        mesh=mesh,
        in_specs=(P(None, "gx", "gy", "cyc"),),
        out_specs=P(None, "gx", "gy", "cyc"),
        check_vma=False,
    )
```

```python
import jax
import jax.numpy as jnp
from jax import lax
from jax.experimental import pallas as pl
from jax.experimental.pallas import tpu as pltpu
from jax.sharding import PartitionSpec as P

RANK = 128
F32 = jnp.float32
BF = jnp.bfloat16

HIGH = lax.Precision.HIGHEST


def mm(a,b,ca,cb):
    return lax.dot_general(a,b,(((ca,),(cb,)),((),())),precision=HIGH,preferred_element_type=F32)

def thirds(v):
    top = v.astype(BF).astype(F32)
    rest = v - top
    mid = rest.astype(BF).astype(F32)
    return top, mid, rest - mid

def small_inverse(entry, n):
    d=[row[:] for row in entry]
    l=[[None]*n for _ in range(n)]
    r=[None]*n
    for j in range(n):
        g=lax.rsqrt(d[j][j])
        g=g*(1.5-(0.5*d[j][j])*(g*g))
        r[j]=g
        for i in range(j+1,n): l[i][j]=d[i][j]*g
        for k in range(j+1,n):
            for i in range(k,n): d[i][k]=d[i][k]-l[i][j]*l[k][j]
    x=[[None]*n for _ in range(n)]
    for j in range(n):
        x[j][j]=r[j]
        for i in range(j+1,n):
            t=l[i][j]*x[j][j]
            for k in range(j+1,i): t=t+l[i][k]*x[k][j]
            x[i][j]=-(t*r[i])
    return x

def inverse_factor(work, n):
    step=8
    sub=lax.broadcasted_iota(jnp.int32,(step,n),0)
    for at in range(0,n,step):
        rows=work[at:at+step,:]
        block=rows[:,at:at+step]
        entry=[[jnp.broadcast_to(block[i:i+1,j:j+1],(step,n)) for j in range(i+1)] for i in range(step)]
        x=small_inverse(entry,step)
        left=jnp.zeros((step,n),F32); right=jnp.zeros((step,n),F32)
        for j in range(step):
            col=x[j][j]
            for i in range(j+1,step): col=jnp.where(sub>=i,x[i][j],col)
            col=jnp.where(sub<j,0.0,col)
            left=left+col*jnp.broadcast_to(rows[j:j+1,:n],(step,n))
            right=right+col*jnp.broadcast_to(rows[j:j+1,n:],(step,n))
        new=jnp.concatenate([left,right],axis=1)
        work[at:at+step,:]=new
        if at+step<n:
            a,b,c=thirds(new)
            lhs=jnp.concatenate([a[:,:n],a[:,:n],a[:,:n],b[:,:n],b[:,:n],c[:,:n]],axis=0).astype(BF)
            rhs=jnp.concatenate([a,b,c,a,b,a],axis=0).astype(BF)
            prod=lax.dot_general(lhs,rhs,(((0,),(0,)),((),())),preferred_element_type=F32)
            work[at+step:,:]=work[at+step:,:]-prod[at+step:,:]

def eye(n):
    return (lax.broadcasted_iota(jnp.int32,(n,n),0)==lax.broadcasted_iota(jnp.int32,(n,n),1)).astype(F32)

def vectors_body(h, work, moved):
    w=h.shape[0]; n=w//2
    on=lax.broadcasted_iota(jnp.int32,(w,w),0)==lax.broadcasted_iota(jnp.int32,(w,w),1)
    trace=jnp.sum(jnp.where(on,h,0.0))
    hn=h*(1.0/(trace/w+1e-06))
    moved[...]=mm(hn,hn[:,:n]+hn[:,n:],1,0)
    identity=eye(n)
    for turn in range(2):
        z=moved[...]
        gram=mm(z,z,0,0)
        if turn==0:
            gram=gram+identity*(jnp.sum(gram*identity)*(4e-7))
        work[:,:n]=gram
        work[:,n:]=identity
        inverse_factor(work,n)
        v=mm(z,work[:,n:],1,1)
        if turn==0:
            moved[...]=mm(hn,v,1,0)
    return v

def first_kernel(g_ref, v_ref, n_ref, work, moved):
    h=g_ref[...]
    v=vectors_body(h,work,moved)
    v_ref[...]=v
    n_ref[...]=mm(v,mm(h,v,1,0),0,0)

def first(gram):
    w=gram.shape[0]
    return pl.pallas_call(first_kernel,
        out_shape=(jax.ShapeDtypeStruct((w,RANK),F32),jax.ShapeDtypeStruct((RANK,RANK),F32)),
        scratch_shapes=[pltpu.VMEM((RANK,2*RANK),F32),pltpu.VMEM((w,RANK),F32)])(gram)


def edges(block, axis, dim):
    count = lax.axis_size(axis)
    forward = [(i, i + 1) for i in range(count - 1)]
    backward = [(target, source) for source, target in forward]
    low = lax.ppermute(
        lax.slice_in_dim(block, block.shape[dim] - 1, None, axis=dim), axis, forward
    )
    high = lax.ppermute(lax.slice_in_dim(block, 0, 1, axis=dim), axis, backward)
    return low, high


def swapped(value, axis, stride):
    mask = 2**stride
    pairs = [(source, source ^ mask) for source in range(lax.axis_size(axis))]
    return lax.ppermute(value, axis, pairs)


def scatter_sum(value, axis):
    count = lax.axis_size(axis)
    parts = lax.all_to_all(value, axis, 0, 0, tiled=True)
    return parts.reshape(count, -1, value.shape[1]).sum(0)


def gathered(value, axis):
    count = lax.axis_size(axis)
    copies = jnp.broadcast_to(value[None], (count,) + value.shape)
    return lax.all_to_all(copies.reshape(-1, value.shape[1]), axis, 0, 0, tiled=True)


def all_sum(value):
    flat = value.reshape(-1, 128)
    part = scatter_sum(flat, "gx")
    part = gathered(part, "gy").reshape(lax.axis_size("gy"), -1, 128).sum(0)
    return gathered(part, "gx").reshape(value.shape)


def strain_rows(block):
    x_low, x_high = edges(block, "gx", 1)
    y_low, y_high = edges(block, "gy", 2)
    field = block.astype(jnp.float32)
    x_pad = jnp.concatenate([x_low, block, x_high], axis=1).astype(jnp.float32)
    y_pad = jnp.concatenate([y_low, block, y_high], axis=2).astype(jnp.float32)
    along_x = (x_pad[:, 2:] - x_pad[:, :-2]) * 0.5
    along_y = (y_pad[:, :, 2:] - y_pad[:, :, :-2]) * 0.5
    strain_xx = along_x[0]
    strain_yy = along_y[1]
    strain_xy = 0.5 * (along_x[1] + along_y[0])
    first = strain_xx + strain_yy
    second = strain_xx * strain_yy - strain_xy * strain_xy
    return jnp.stack([first, second]).reshape(-1, field.shape[-1])


def gram_of(joined):
    return lax.dot_general(
        joined,
        joined,
        (((0,), (0,)), ((), ())),
        precision=lax.Precision.HIGHEST,
        preferred_element_type=jnp.float32,
    )


def matmul_high(left, right):
    return jnp.dot(left, right, precision=lax.Precision.HIGHEST, preferred_element_type=jnp.float32)


def vectors_of(gram):
    return first(gram)[0]


def finish(joined, gram):
    return matmul_high(joined, vectors_of(gram))


def truncate(joined):
    return finish(joined, all_sum(gram_of(joined)))


def own_columns(whole):
    groups = lax.axis_size("cyc")
    share = whole.shape[1] // groups
    return lax.dynamic_slice_in_dim(whole, lax.axis_index("cyc") * share, share, 1)


def on_device(displacement):
    local_rows = displacement.shape[1]
    local_cols = displacement.shape[2]
    piece = truncate(strain_rows(displacement))
    group = lax.axis_index("cyc")
    for level in range(lax.axis_size("cyc").bit_length() - 1):
        partner = swapped(piece, "cyc", level)
        is_low = group >> level & 1 == 0
        first_half = jnp.where(is_low, piece, partner)
        second_half = jnp.where(is_low, partner, piece)
        piece = truncate(jnp.concatenate([first_half, second_half], axis=1))
    result = own_columns(piece)
    return result.reshape(2, local_rows, local_cols, result.shape[1])


def solution(mesh):
    return jax.shard_map(
        on_device,
        mesh=mesh,
        in_specs=(P(None, "gx", "gy", "cyc"),),
        out_specs=P(None, "gx", "gy", "cyc"),
        check_vma=False,
    )
```

```python
import jax
import jax.numpy as jnp
from jax import lax
from jax.experimental import pallas as pl
from jax.experimental.pallas import tpu as pltpu
from jax.sharding import PartitionSpec as P

RANK = 128
F32 = jnp.float32
BF = jnp.bfloat16
HIGH = lax.Precision.HIGHEST
ROWS = 4
LIMIT = 56 * 2**20


def mm(a, b, ca, cb):
    return lax.dot_general(
        a, b, (((ca,), (cb,)), ((), ())), precision=HIGH, preferred_element_type=F32
    )


def fast(a, b, ca, cb):
    return lax.dot_general(a, b, (((ca,), (cb,)), ((), ())), preferred_element_type=F32)


def thirds(v):
    top = v.astype(BF).astype(F32)
    rest = v - top
    mid = rest.astype(BF).astype(F32)
    return top, mid, rest - mid


def small_inverse(entry, n):
    d = [row[:] for row in entry]
    l = [[None] * n for _ in range(n)]
    r = [None] * n
    for j in range(n):
        g = lax.rsqrt(d[j][j])
        g = g * (1.5 - (0.5 * d[j][j]) * (g * g))
        r[j] = g
        for i in range(j + 1, n):
            l[i][j] = d[i][j] * g
        for k in range(j + 1, n):
            for i in range(k, n):
                d[i][k] = d[i][k] - l[i][j] * l[k][j]
    x = [[None] * n for _ in range(n)]
    for j in range(n):
        x[j][j] = r[j]
        for i in range(j + 1, n):
            t = l[i][j] * x[j][j]
            for k in range(j + 1, i):
                t = t + l[i][k] * x[k][j]
            x[i][j] = -(t * r[i])
    return x


def inverse_factor(work, n):
    step = 8
    sub = lax.broadcasted_iota(jnp.int32, (step, n), 0)
    for at in range(0, n, step):
        rows = work[at : at + step, :]
        block = rows[:, at : at + step]
        entry = [
            [jnp.broadcast_to(block[i : i + 1, j : j + 1], (step, n)) for j in range(i + 1)]
            for i in range(step)
        ]
        x = small_inverse(entry, step)
        left = jnp.zeros((step, n), F32)
        right = jnp.zeros((step, n), F32)
        for j in range(step):
            col = x[j][j]
            for i in range(j + 1, step):
                col = jnp.where(sub >= i, x[i][j], col)
            col = jnp.where(sub < j, 0.0, col)
            left = left + col * jnp.broadcast_to(rows[j : j + 1, :n], (step, n))
            right = right + col * jnp.broadcast_to(rows[j : j + 1, n:], (step, n))
        new = jnp.concatenate([left, right], axis=1)
        work[at : at + step, :] = new
        if at + step < n:
            a, b, c = thirds(new)
            lhs = jnp.concatenate([a, a, a, b, b, c], axis=0)[:, :n].astype(BF)
            rhs = jnp.concatenate([a, b, c, a, b, a], axis=0).astype(BF)
            prod = fast(lhs, rhs, 0, 0)
            work[at + step :, :] = work[at + step :, :] - prod[at + step :, :]


def eye(n):
    row = lax.broadcasted_iota(jnp.int32, (n, n), 0)
    return (row == lax.broadcasted_iota(jnp.int32, (n, n), 1)).astype(F32)


def vectors_of(h, work, moved, found):
    w = h.shape[0]
    n = w // 2
    identity = eye(n)
    trace = jnp.sum(h[:n, :n] * identity) + jnp.sum(h[n:, n:] * identity)
    hn = h * (1.0 / (trace / w + 1e-06))
    moved[...] = mm(hn, hn[:, :n] + hn[:, n:], 1, 0)

    def turn(at, carry):
        z = moved[...]
        gram = mm(z, z, 0, 0)
        shift = jnp.where(at == 0, 4e-7, 0.0)
        work[:, :n] = gram + identity * (jnp.sum(gram * identity) * shift)
        work[:, n:] = identity
        inverse_factor(work, n)
        v = mm(z, work[:, n:], 1, 1)
        found[...] = v
        moved[...] = mm(hn, v, 1, 0)
        return carry

    lax.fori_loop(0, 2, turn, 0)
    return found[...]


def first_kernel(g_ref, out_ref, work, moved, found):
    h = joined_gram(g_ref[:RANK], g_ref[RANK : 2 * RANK], g_ref[2 * RANK :])
    w = h.shape[0]
    v = vectors_of(h, work, moved, found)
    out_ref[:w] = v
    out_ref[w:] = mm(v, mm(h, v, 1, 0), 0, 0)


def scratch():
    return [
        pltpu.VMEM((RANK, 2 * RANK), F32),
        pltpu.VMEM((2 * RANK, RANK), F32),
        pltpu.VMEM((2 * RANK, RANK), F32),
    ]


def first_level(gram):
    return pl.pallas_call(
        first_kernel,
        out_shape=jax.ShapeDtypeStruct((3 * RANK, RANK), F32),
        scratch_shapes=scratch(),
    )(gram)


def joined_gram(own_gram, cross, far_gram):
    top = jnp.concatenate([own_gram, cross], axis=1)
    low = jnp.concatenate([cross.T, far_gram], axis=1)
    return jnp.concatenate([top, low], axis=0)


def level_kernel(own_ref, cross_ref, far_ref, out_ref, work, moved, found):
    w = own_ref.shape[0] - RANK
    h = joined_gram(own_ref[w:], cross_ref[...], far_ref[w:])
    u = vectors_of(h, work, moved, found)
    out_ref[:w] = mm(own_ref[:w], u[:RANK], 1, 0)
    out_ref[w : 2 * w] = mm(far_ref[:w], u[RANK:], 1, 0)
    out_ref[2 * w :] = mm(u, mm(h, u, 1, 0), 0, 0)


def next_level(own, cross, far):
    w = own.shape[0] - RANK
    return pl.pallas_call(
        level_kernel,
        out_shape=jax.ShapeDtypeStruct((2 * w + RANK, RANK), F32),
        scratch_shapes=scratch(),
    )(own, cross, far)


def last_kernel(own_ref, cross_ref, far_ref, pick_ref, out_ref, work, moved, found):
    w = own_ref.shape[0] - RANK
    h = joined_gram(own_ref[w:], cross_ref[...], far_ref[w:])
    u = vectors_of(h, work, moved, found)
    share = pick_ref.shape[0]
    for at, ref in ((0, own_ref), (1, far_ref)):
        mine = mm(pick_ref[...], u[at * RANK : (at + 1) * RANK], 1, 1)
        part = mm(mine, ref[:w], 1, 1)
        top = part.astype(BF)
        out_ref[:share, at * w : (at + 1) * w] = top
        out_ref[share:, at * w : (at + 1) * w] = (part - top.astype(F32)).astype(BF)


def last_level(own, cross, far, pick):
    w = own.shape[0] - RANK
    return pl.pallas_call(
        last_kernel,
        out_shape=jax.ShapeDtypeStruct((2 * pick.shape[0], 2 * w), BF),
        scratch_shapes=scratch(),
    )(own, cross, far, pick)


def project_kernel(own_ref, far_ref, *refs):
    *blocks, o_ref = refs
    w = own_ref.shape[0] - RANK
    own = own_ref[:w]
    total = jnp.zeros(o_ref.shape, F32)
    for g, block in enumerate(blocks):
        snaps = block.shape[0]
        seen = mm(block[...], own, 1, 0)
        total += mm(seen, far_ref[g * snaps : (g + 1) * snaps], 0, 0)
    o_ref[...] = total


def project(own, far, blocks):
    return pl.pallas_call(project_kernel, out_shape=jax.ShapeDtypeStruct((RANK, RANK), F32))(
        own, far, *blocks
    )


def feature_kernel(count, u_ref, halo_ref, *refs):
    left = refs[: 2 * count]
    hi_ref, lo_ref, gram_ref, field, sides, sums = refs[2 * count :]
    at = pl.program_id(0)
    _, height, wide, snaps = u_ref.shape

    @pl.when(at == 0)
    def _():
        sides[...] = halo_ref[:, :, wide:, :].astype(F32)
        field[:, 0] = halo_ref[:, 0, :wide, :].astype(F32)
        field[:, height + 1] = halo_ref[:, 1, :wide, :].astype(F32)
        field[:, 1] = u_ref[:, 0].astype(F32)
        sums[...] = jnp.zeros_like(sums)

    edge = lax.broadcasted_iota(jnp.int32, (wide, 128), 0)

    def one(r, carry):
        i = at * ROWS + r

        @pl.when(i + 1 < height)
        def _():
            field[:, i + 2] = u_ref[:, i + 1].astype(F32)

        for start in range(0, snaps, 128):
            lanes = slice(start, start + 128)

            def along_x(c):
                return field[c, i + 2, :, lanes] - field[c, i, :, lanes]

            def along_y(c):
                here = field[c, i + 1, :, lanes]
                back = jnp.where(
                    edge == 0, sides[c, 0, pl.ds(i, 1), :][:, lanes], pltpu.roll(here, 1, 0)
                )
                ahead = jnp.where(
                    edge == wide - 1,
                    sides[c, 1, pl.ds(i, 1), :][:, lanes],
                    pltpu.roll(here, wide - 1, 0),
                )
                return ahead - back

            strain_xx = along_x(0)
            strain_yy = along_y(1)
            shear = along_x(1) + along_y(0)
            values = (
                0.5 * (strain_xx + strain_yy),
                0.25 * (strain_xx * strain_yy) - 0.0625 * (shear * shear),
            )
            span = pl.ds(pl.multiple_of(r * wide, wide), wide)
            for k, value in enumerate(values):
                hi = value.astype(BF)
                hi_ref[k, span, lanes] = hi
                lo_ref[k, span, lanes] = (value - hi.astype(F32)).astype(BF)
        return carry

    lax.fori_loop(0, ROWS, one, 0)
    for k in range(2):
        hi = hi_ref[k]
        lo = lo_ref[k]
        if count == 0:
            sums[:, :snaps] += fast(hi, hi, 0, 0)
            sums[:, snaps:] += fast(hi, lo, 0, 0)
        for g in range(count):
            other = left[2 * g][k]
            rest = left[2 * g + 1][k]
            sums[:, g * snaps : (g + 1) * snaps] += (
                fast(hi, other, 0, 0) + fast(hi, rest, 0, 0) + fast(lo, other, 0, 0)
            )

    @pl.when(at == pl.num_programs(0) - 1)
    def _():
        if count == 0:
            mixed = sums[:, snaps:]
            total = sums[:, :snaps] + (mixed + mixed.T)
            gram_ref[:RANK] = total[:RANK, :RANK]
            gram_ref[RANK : 2 * RANK] = total[:RANK, RANK:]
            gram_ref[2 * RANK :] = total[RANK:, RANK:]
        else:
            gram_ref[...] = sums[:, : count * snaps]


def features(u, halo, lefts):
    _, height, wide, snaps = u.shape
    count = len(lefts)
    full = lambda array: pl.BlockSpec(array.shape, lambda i: (0,) * array.ndim)
    part = pl.BlockSpec((2, ROWS * wide, snaps), lambda i: (0, i, 0))
    half = jax.ShapeDtypeStruct((2, height * wide, snaps), BF)
    shape = (snaps, count * snaps) if count else (3 * RANK, RANK)
    hi, lo, gram = pl.pallas_call(
        lambda *refs: feature_kernel(count, *refs),
        grid=(height // ROWS,),
        in_specs=[full(u), full(halo)] + [part] * (2 * count),
        out_specs=(part, part, pl.BlockSpec(shape, lambda i: (0, 0))),
        out_shape=(half, half, jax.ShapeDtypeStruct(shape, F32)),
        scratch_shapes=[
            pltpu.VMEM((2, height + 2, wide, snaps), F32),
            pltpu.VMEM((2, 2, height, snaps), F32),
            pltpu.VMEM((snaps, max(count, 2) * snaps), F32),
        ],
        compiler_params=pltpu.CompilerParams(vmem_limit_bytes=LIMIT),
    )(u, halo, *[array for pair in lefts for array in pair])
    return (hi, lo), gram


def finish_kernel(*refs):
    *halves, w_ref, o_ref = refs
    groups = len(halves) // 2
    snaps = w_ref.shape[1] // groups
    share = w_ref.shape[0] // 2
    wide = o_ref.shape[-1]
    total = jnp.zeros((share, halves[0].shape[1]), F32)
    for g in range(groups):
        w = w_ref[:, g * snaps : (g + 1) * snaps]
        both = fast(w, halves[2 * g][0], 1, 1)
        total += both[:share] + both[share:]
        total += fast(w[:share], halves[2 * g + 1][0], 1, 1)
    for r in range(o_ref.shape[1]):
        o_ref[0, r] = total[:, r * wide : (r + 1) * wide]


def finish(pairs, weights, height, wide):
    rows = 8
    _, _, snaps = pairs[0][0].shape
    share = weights.shape[0] // 2
    part = pl.BlockSpec((1, rows * wide, snaps), lambda k, i: (k, i, 0))
    return pl.pallas_call(
        finish_kernel,
        grid=(2, height // rows),
        in_specs=[part] * (2 * len(pairs))
        + [pl.BlockSpec(weights.shape, lambda k, i: (0, 0))],
        out_specs=pl.BlockSpec((1, rows, share, wide), lambda k, i: (k, i, 0, 0)),
        out_shape=jax.ShapeDtypeStruct((2, height, share, wide), F32),
        compiler_params=pltpu.CompilerParams(vmem_limit_bytes=LIMIT),
    )(*[array for pair in pairs for array in pair], weights)


def edges(block, axis, dim):
    count = lax.axis_size(axis)
    forward = [(i, i + 1) for i in range(count - 1)]
    backward = [(target, source) for source, target in forward]
    low = lax.ppermute(
        lax.slice_in_dim(block, block.shape[dim] - 1, None, axis=dim), axis, forward
    )
    high = lax.ppermute(lax.slice_in_dim(block, 0, 1, axis=dim), axis, backward)
    return low, high


def halo_of(block):
    _, height, wide, snaps = block.shape
    x_low, x_high = edges(block, "gx", 1)
    y_low, y_high = edges(block, "gy", 2)
    low = jnp.concatenate([x_low[:, 0], y_low[:, :, 0]], axis=1)
    high = jnp.concatenate([x_high[:, 0], y_high[:, :, 0]], axis=1)
    return jnp.stack([low, high], axis=1)


def swapped(value, mask):
    pairs = [(source, source ^ mask) for source in range(lax.axis_size("cyc"))]
    return lax.ppermute(value, "cyc", pairs)


def scatter_sum(value, axis):
    count = lax.axis_size(axis)
    parts = lax.all_to_all(value, axis, 0, 0, tiled=True)
    return parts.reshape(count, -1, value.shape[1]).sum(0)


def gathered(value, axis):
    count = lax.axis_size(axis)
    copies = jnp.broadcast_to(value[None], (count,) + value.shape)
    return lax.all_to_all(copies.reshape(-1, value.shape[1]), axis, 0, 0, tiled=True)


def all_sum(value):
    flat = value.reshape(-1, 128)
    part = scatter_sum(flat, "gx")
    part = gathered(part, "gy").reshape(lax.axis_size("gy"), -1, 128).sum(0)
    return gathered(part, "gx").reshape(value.shape)


def on_device(displacement):
    _, height, wide, _ = displacement.shape
    groups = lax.axis_size("cyc")
    halo = halo_of(displacement)
    near = swapped(displacement, 1)
    side = swapped(displacement, 3)
    own, gram = features(displacement, halo, [])
    total = all_sum(gram)
    relayed, _ = lax.optimization_barrier((side, total))
    far = swapped(relayed, 1)
    level0 = first_level(total)
    pair, cross1 = features(near, swapped(halo, 1), [own])
    other0 = swapped(level0, 1)
    level1 = next_level(level0, all_sum(project(level0, other0, [cross1])), other0)
    fourth, cross3 = features(side, swapped(halo, 3), [own, pair])
    third, cross2 = features(far, swapped(halo, 2), [own, pair])
    other1 = swapped(level1, 2)
    share = RANK // groups
    column = lax.axis_index("cyc") * share + jnp.arange(share)
    pick = (column[:, None] == jnp.arange(RANK)[None, :]).astype(F32)
    total = all_sum(project(level1, other1, [cross2, cross3]))
    weights = last_level(level1, total, other1, pick)
    result = finish([own, pair, third, fourth], weights, height, wide)
    return result.transpose(0, 1, 3, 2)


def solution(mesh):
    return jax.shard_map(
        on_device,
        mesh=mesh,
        in_specs=(P(None, "gx", "gy", "cyc"),),
        out_specs=P(None, "gx", "gy", "cyc"),
        check_vma=False,
    )
```

```python
import jax
import jax.numpy as jnp
from jax import lax
from jax.experimental import pallas as pl
from jax.experimental.pallas import tpu as pltpu
from jax.sharding import PartitionSpec as P

RANK = 128
F32 = jnp.float32
BF = jnp.bfloat16
HIGH = lax.Precision.HIGHEST
ROWS = 4
LIMIT = 56 * 2**20


def mm(a, b, ca, cb):
    return lax.dot_general(
        a, b, (((ca,), (cb,)), ((), ())), precision=HIGH, preferred_element_type=F32
    )


def fast(a, b, ca, cb):
    return lax.dot_general(a, b, (((ca,), (cb,)), ((), ())), preferred_element_type=F32)


def thirds(v):
    top = v.astype(BF).astype(F32)
    rest = v - top
    mid = rest.astype(BF).astype(F32)
    return top, mid, rest - mid


def small_inverse(entry, n):
    d = [row[:] for row in entry]
    l = [[None] * n for _ in range(n)]
    r = [None] * n
    for j in range(n):
        g = lax.rsqrt(d[j][j])
        g = g * (1.5 - (0.5 * d[j][j]) * (g * g))
        r[j] = g
        for i in range(j + 1, n):
            l[i][j] = d[i][j] * g
        for k in range(j + 1, n):
            for i in range(k, n):
                d[i][k] = d[i][k] - l[i][j] * l[k][j]
    x = [[None] * n for _ in range(n)]
    for j in range(n):
        x[j][j] = r[j]
        for i in range(j + 1, n):
            t = l[i][j] * x[j][j]
            for k in range(j + 1, i):
                t = t + l[i][k] * x[k][j]
            x[i][j] = -(t * r[i])
    return x


def inverse_factor(work, n):
    step = 8
    sub = lax.broadcasted_iota(jnp.int32, (step, n), 0)
    for at in range(0, n, step):
        rows = work[at : at + step, :]
        block = rows[:, at : at + step]
        entry = [
            [jnp.broadcast_to(block[i : i + 1, j : j + 1], (step, n)) for j in range(i + 1)]
            for i in range(step)
        ]
        x = small_inverse(entry, step)
        left = jnp.zeros((step, n), F32)
        right = jnp.zeros((step, n), F32)
        for j in range(step):
            col = x[j][j]
            for i in range(j + 1, step):
                col = jnp.where(sub >= i, x[i][j], col)
            col = jnp.where(sub < j, 0.0, col)
            left = left + col * jnp.broadcast_to(rows[j : j + 1, :n], (step, n))
            right = right + col * jnp.broadcast_to(rows[j : j + 1, n:], (step, n))
        new = jnp.concatenate([left, right], axis=1)
        work[at : at + step, :] = new
        if at + step < n:
            a, b, c = thirds(new)
            lhs = jnp.concatenate([a, a, a, b, b, c], axis=0)[:, :n].astype(BF)
            rhs = jnp.concatenate([a, b, c, a, b, a], axis=0).astype(BF)
            prod = fast(lhs, rhs, 0, 0)
            work[at + step :, :] = work[at + step :, :] - prod[at + step :, :]


def eye(n):
    row = lax.broadcasted_iota(jnp.int32, (n, n), 0)
    return (row == lax.broadcasted_iota(jnp.int32, (n, n), 1)).astype(F32)


def vectors_of(h, work, moved, found):
    w = h.shape[0]
    n = w // 2
    identity = eye(n)
    trace = jnp.sum(h[:n, :n] * identity) + jnp.sum(h[n:, n:] * identity)
    hn = h * (1.0 / (trace / w + 1e-06))
    moved[...] = mm(hn, hn[:, :n] + hn[:, n:], 1, 0)

    def turn(at, carry):
        z = moved[...]
        gram = mm(z, z, 0, 0)
        shift = jnp.where(at == 0, 4e-7, 0.0)
        work[:, :n] = gram + identity * (jnp.sum(gram * identity) * shift)
        work[:, n:] = identity
        inverse_factor(work, n)
        v = mm(z, work[:, n:], 1, 1)
        found[...] = v
        moved[...] = mm(hn, v, 1, 0)
        return carry

    lax.fori_loop(0, 2, turn, 0)
    return found[...]


def first_kernel(g_ref, out_ref, work, moved, found):
    h = joined_gram(g_ref[:RANK], g_ref[RANK : 2 * RANK], g_ref[2 * RANK :])
    w = h.shape[0]
    v = vectors_of(h, work, moved, found)
    out_ref[:w] = v
    out_ref[w:] = mm(v, mm(h, v, 1, 0), 0, 0)


def scratch():
    return [
        pltpu.VMEM((RANK, 2 * RANK), F32),
        pltpu.VMEM((2 * RANK, RANK), F32),
        pltpu.VMEM((2 * RANK, RANK), F32),
    ]


def first_level(gram):
    return pl.pallas_call(
        first_kernel,
        out_shape=jax.ShapeDtypeStruct((3 * RANK, RANK), F32),
        scratch_shapes=scratch(),
    )(gram)


def joined_gram(own_gram, cross, far_gram):
    top = jnp.concatenate([own_gram, cross], axis=1)
    low = jnp.concatenate([cross.T, far_gram], axis=1)
    return jnp.concatenate([top, low], axis=0)


def level_kernel(own_ref, cross_ref, far_ref, out_ref, work, moved, found):
    w = own_ref.shape[0] - RANK
    h = joined_gram(own_ref[w:], cross_ref[...], far_ref[w:])
    u = vectors_of(h, work, moved, found)
    out_ref[:w] = mm(own_ref[:w], u[:RANK], 1, 0)
    out_ref[w : 2 * w] = mm(far_ref[:w], u[RANK:], 1, 0)
    out_ref[2 * w :] = mm(u, mm(h, u, 1, 0), 0, 0)


def next_level(own, cross, far):
    w = own.shape[0] - RANK
    return pl.pallas_call(
        level_kernel,
        out_shape=jax.ShapeDtypeStruct((2 * w + RANK, RANK), F32),
        scratch_shapes=scratch(),
    )(own, cross, far)


def last_kernel(own_ref, cross_ref, far_ref, pick_ref, out_ref, work, moved, found):
    w = own_ref.shape[0] - RANK
    h = joined_gram(own_ref[w:], cross_ref[...], far_ref[w:])
    u = vectors_of(h, work, moved, found)
    share = pick_ref.shape[0]
    for at, ref in ((0, own_ref), (1, far_ref)):
        mine = mm(pick_ref[...], u[at * RANK : (at + 1) * RANK], 1, 1)
        part = mm(mine, ref[:w], 1, 1)
        top = part.astype(BF)
        out_ref[:share, at * w : (at + 1) * w] = top
        out_ref[share:, at * w : (at + 1) * w] = (part - top.astype(F32)).astype(BF)


def last_level(own, cross, far, pick):
    w = own.shape[0] - RANK
    return pl.pallas_call(
        last_kernel,
        out_shape=jax.ShapeDtypeStruct((2 * pick.shape[0], 2 * w), BF),
        scratch_shapes=scratch(),
    )(own, cross, far, pick)


def project_kernel(own_ref, far_ref, *refs):
    *blocks, o_ref = refs
    w = own_ref.shape[0] - RANK
    own = own_ref[:w]
    total = jnp.zeros(o_ref.shape, F32)
    for g, block in enumerate(blocks):
        snaps = block.shape[0]
        seen = mm(block[...], own, 1, 0)
        total += mm(seen, far_ref[g * snaps : (g + 1) * snaps], 0, 0)
    o_ref[...] = total


def project(own, far, blocks):
    return pl.pallas_call(project_kernel, out_shape=jax.ShapeDtypeStruct((RANK, RANK), F32))(
        own, far, *blocks
    )


def feature_kernel(count, u_ref, halo_ref, *refs):
    left = refs[: 2 * count]
    hi_ref, lo_ref, gram_ref, field, sides, sums = refs[2 * count :]
    at = pl.program_id(0)
    _, height, wide, snaps = u_ref.shape

    @pl.when(at == 0)
    def _():
        sides[...] = halo_ref[:, :, wide:, :].astype(F32)
        field[:, 0] = halo_ref[:, 0, :wide, :].astype(F32)
        field[:, height + 1] = halo_ref[:, 1, :wide, :].astype(F32)
        field[:, 1] = u_ref[:, 0].astype(F32)
        sums[...] = jnp.zeros_like(sums)

    edge = lax.broadcasted_iota(jnp.int32, (wide, 128), 0)

    def one(r, carry):
        i = at * ROWS + r

        @pl.when(i + 1 < height)
        def _():
            field[:, i + 2] = u_ref[:, i + 1].astype(F32)

        for start in range(0, snaps, 128):
            lanes = slice(start, start + 128)

            def along_x(c):
                return field[c, i + 2, :, lanes] - field[c, i, :, lanes]

            def along_y(c):
                here = field[c, i + 1, :, lanes]
                back = jnp.where(
                    edge == 0, sides[c, 0, pl.ds(i, 1), :][:, lanes], pltpu.roll(here, 1, 0)
                )
                ahead = jnp.where(
                    edge == wide - 1,
                    sides[c, 1, pl.ds(i, 1), :][:, lanes],
                    pltpu.roll(here, wide - 1, 0),
                )
                return ahead - back

            strain_xx = along_x(0)
            strain_yy = along_y(1)
            shear = along_x(1) + along_y(0)
            values = (
                0.5 * (strain_xx + strain_yy),
                0.25 * (strain_xx * strain_yy) - 0.0625 * (shear * shear),
            )
            span = pl.ds(pl.multiple_of(r * wide, wide), wide)
            for k, value in enumerate(values):
                hi = value.astype(BF)
                hi_ref[k, span, lanes] = hi
                lo_ref[k, span, lanes] = (value - hi.astype(F32)).astype(BF)
        return carry

    lax.fori_loop(0, ROWS, one, 0)
    for k in range(2):
        hi = hi_ref[k]
        lo = lo_ref[k]
        if count == 0:
            sums[:, :snaps] += fast(hi, hi, 0, 0)
            sums[:, snaps:] += fast(hi, lo, 0, 0)
        for g in range(count):
            other = left[2 * g][k]
            rest = left[2 * g + 1][k]
            sums[:, g * snaps : (g + 1) * snaps] += (
                fast(hi, other, 0, 0) + fast(hi, rest, 0, 0) + fast(lo, other, 0, 0)
            )

    @pl.when(at == pl.num_programs(0) - 1)
    def _():
        if count == 0:
            mixed = sums[:, snaps:]
            total = sums[:, :snaps] + (mixed + mixed.T)
            gram_ref[:RANK] = total[:RANK, :RANK]
            gram_ref[RANK : 2 * RANK] = total[:RANK, RANK:]
            gram_ref[2 * RANK :] = total[RANK:, RANK:]
        else:
            gram_ref[...] = sums[:, : count * snaps]


def features(u, halo, lefts):
    _, height, wide, snaps = u.shape
    count = len(lefts)
    full = lambda array: pl.BlockSpec(array.shape, lambda i: (0,) * array.ndim)
    part = pl.BlockSpec((2, ROWS * wide, snaps), lambda i: (0, i, 0))
    half = jax.ShapeDtypeStruct((2, height * wide, snaps), BF)
    shape = (snaps, count * snaps) if count else (3 * RANK, RANK)
    hi, lo, gram = pl.pallas_call(
        lambda *refs: feature_kernel(count, *refs),
        grid=(height // ROWS,),
        in_specs=[full(u), full(halo)] + [part] * (2 * count),
        out_specs=(part, part, pl.BlockSpec(shape, lambda i: (0, 0))),
        out_shape=(half, half, jax.ShapeDtypeStruct(shape, F32)),
        scratch_shapes=[
            pltpu.VMEM((2, height + 2, wide, snaps), F32),
            pltpu.VMEM((2, 2, height, snaps), F32),
            pltpu.VMEM((snaps, max(count, 2) * snaps), F32),
        ],
        compiler_params=pltpu.CompilerParams(vmem_limit_bytes=LIMIT),
    )(u, halo, *[array for pair in lefts for array in pair])
    return (hi, lo), gram


def finish_kernel(*refs):
    *halves, w_ref, o_ref = refs
    groups = len(halves) // 2
    snaps = w_ref.shape[1] // groups
    share = w_ref.shape[0] // 2
    wide = o_ref.shape[-1]
    total = jnp.zeros((share, halves[0].shape[1]), F32)
    for g in range(groups):
        w = w_ref[:, g * snaps : (g + 1) * snaps]
        both = fast(w, halves[2 * g][0], 1, 1)
        total += both[:share] + both[share:]
        total += fast(w[:share], halves[2 * g + 1][0], 1, 1)
    for r in range(o_ref.shape[1]):
        o_ref[0, r] = total[:, r * wide : (r + 1) * wide]


def finish(pairs, weights, height, wide):
    rows = 8
    _, _, snaps = pairs[0][0].shape
    share = weights.shape[0] // 2
    part = pl.BlockSpec((1, rows * wide, snaps), lambda k, i: (k, i, 0))
    return pl.pallas_call(
        finish_kernel,
        grid=(2, height // rows),
        in_specs=[part] * (2 * len(pairs))
        + [pl.BlockSpec(weights.shape, lambda k, i: (0, 0))],
        out_specs=pl.BlockSpec((1, rows, share, wide), lambda k, i: (k, i, 0, 0)),
        out_shape=jax.ShapeDtypeStruct((2, height, share, wide), F32),
        compiler_params=pltpu.CompilerParams(vmem_limit_bytes=LIMIT),
    )(*[array for pair in pairs for array in pair], weights)


def edges(block, axis, dim):
    count = lax.axis_size(axis)
    forward = [(i, i + 1) for i in range(count - 1)]
    backward = [(target, source) for source, target in forward]
    low = lax.ppermute(
        lax.slice_in_dim(block, block.shape[dim] - 1, None, axis=dim), axis, forward
    )
    high = lax.ppermute(lax.slice_in_dim(block, 0, 1, axis=dim), axis, backward)
    return low, high


def halo_of(block):
    x_low, x_high = edges(block, "gx", 1)
    y_low, y_high = edges(block, "gy", 2)
    low = jnp.concatenate([x_low[:, 0], y_low[:, :, 0]], axis=1)
    high = jnp.concatenate([x_high[:, 0], y_high[:, :, 0]], axis=1)
    return jnp.stack([low, high], axis=1)


def swapped(value, mask):
    pairs = [(source, source ^ mask) for source in range(lax.axis_size("cyc"))]
    return lax.ppermute(value, "cyc", pairs)


def scatter_sum(value, axis):
    count = lax.axis_size(axis)
    parts = lax.all_to_all(value, axis, 0, 0, tiled=True)
    return parts.reshape(count, -1, value.shape[1]).sum(0)


def gathered(value, axis):
    count = lax.axis_size(axis)
    copies = jnp.broadcast_to(value[None], (count,) + value.shape)
    return lax.all_to_all(copies.reshape(-1, value.shape[1]), axis, 0, 0, tiled=True)


def all_sum(value):
    flat = value.reshape(-1, 128)
    part = scatter_sum(flat, "gx")
    part = gathered(part, "gy").reshape(lax.axis_size("gy"), -1, 128).sum(0)
    return gathered(part, "gx").reshape(value.shape)


def whole(displacement):
    _, height, wide, _ = displacement.shape
    groups = lax.axis_size("cyc")
    halo = halo_of(displacement)
    near = swapped(displacement, 1)
    side = swapped(displacement, 3)
    near_halo, far_halo, side_halo = (swapped(halo, mask) for mask in (1, 2, 3))
    own, gram = features(displacement, halo, [])
    total = all_sum(gram)
    level0 = first_level(total)
    other0 = swapped(level0, 1)
    relayed, _ = lax.optimization_barrier((near, total))
    far = swapped(relayed, 3)
    pair, cross1 = features(near, near_halo, [own])
    total = all_sum(project(level0, other0, [cross1]))
    level1 = next_level(level0, total, other0)
    other1 = swapped(level1, 2)
    fourth, cross3 = features(side, side_halo, [own, pair])
    third, cross2 = features(far, far_halo, [own, pair])
    share = RANK // groups
    column = lax.axis_index("cyc") * share + jnp.arange(share)
    pick = (column[:, None] == jnp.arange(RANK)[None, :]).astype(F32)
    total = all_sum(project(level1, other1, [cross2, cross3]))
    weights = last_level(level1, total, other1, pick)
    result = finish([own, pair, third, fourth], weights, height, wide)
    return result.transpose(0, 1, 3, 2)


def solution(mesh):
    return jax.shard_map(
        whole,
        mesh=mesh,
        in_specs=(P(None, "gx", "gy", "cyc"),),
        out_specs=P(None, "gx", "gy", "cyc"),
        check_vma=False,
    )
```

```python
import jax
import jax.numpy as jnp
from jax import lax
from jax.experimental import pallas as pl
from jax.experimental.pallas import tpu as pltpu
from jax.sharding import PartitionSpec as P

RANK = 128
F32 = jnp.float32
BF = jnp.bfloat16
HIGH = lax.Precision.HIGHEST
ROWS = 4
PAD = 8
LIMIT = 56 * 2**20


def mm(a, b, ca, cb):
    return lax.dot_general(
        a, b, (((ca,), (cb,)), ((), ())), precision=HIGH, preferred_element_type=F32
    )


def fast(a, b, ca, cb):
    return lax.dot_general(a, b, (((ca,), (cb,)), ((), ())), preferred_element_type=F32)


def thirds(v):
    top = v.astype(BF).astype(F32)
    rest = v - top
    mid = rest.astype(BF).astype(F32)
    return top, mid, rest - mid


def small_inverse(entry, n):
    d = [row[:] for row in entry]
    l = [[None] * n for _ in range(n)]
    r = [None] * n
    for j in range(n):
        g = lax.rsqrt(d[j][j])
        g = g * (1.5 - (0.5 * d[j][j]) * (g * g))
        r[j] = g
        for i in range(j + 1, n):
            l[i][j] = d[i][j] * g
        for k in range(j + 1, n):
            for i in range(k, n):
                d[i][k] = d[i][k] - l[i][j] * l[k][j]
    x = [[None] * n for _ in range(n)]
    for j in range(n):
        x[j][j] = r[j]
        for i in range(j + 1, n):
            t = l[i][j] * x[j][j]
            for k in range(j + 1, i):
                t = t + l[i][k] * x[k][j]
            x[i][j] = -(t * r[i])
    return x


def inverse_factor(work, n):
    step = 8
    sub = lax.broadcasted_iota(jnp.int32, (step, n), 0)
    for at in range(0, n, step):
        rows = work[at : at + step, :]
        block = rows[:, at : at + step]
        entry = [
            [jnp.broadcast_to(block[i : i + 1, j : j + 1], (step, n)) for j in range(i + 1)]
            for i in range(step)
        ]
        x = small_inverse(entry, step)
        left = jnp.zeros((step, n), F32)
        right = jnp.zeros((step, n), F32)
        for j in range(step):
            col = x[j][j]
            for i in range(j + 1, step):
                col = jnp.where(sub >= i, x[i][j], col)
            col = jnp.where(sub < j, 0.0, col)
            left = left + col * jnp.broadcast_to(rows[j : j + 1, :n], (step, n))
            right = right + col * jnp.broadcast_to(rows[j : j + 1, n:], (step, n))
        new = jnp.concatenate([left, right], axis=1)
        work[at : at + step, :] = new
        if at + step < n:
            a, b, c = thirds(new)
            lhs = jnp.concatenate([a, a, a, b, b, c], axis=0)[:, :n].astype(BF)
            rhs = jnp.concatenate([a, b, c, a, b, a], axis=0).astype(BF)
            prod = fast(lhs, rhs, 0, 0)
            work[at + step :, :] = work[at + step :, :] - prod[at + step :, :]


def eye(n):
    row = lax.broadcasted_iota(jnp.int32, (n, n), 0)
    return (row == lax.broadcasted_iota(jnp.int32, (n, n), 1)).astype(F32)


def vectors_of(h, work, moved, found):
    w = h.shape[0]
    n = w // 2
    identity = eye(n)
    trace = jnp.sum(h[:n, :n] * identity) + jnp.sum(h[n:, n:] * identity)
    hn = h * (1.0 / (trace / w + 1e-06))
    moved[...] = mm(hn, hn[:, :n] + hn[:, n:], 1, 0)

    def turn(at, carry):
        z = moved[...]
        gram = mm(z, z, 0, 0)
        shift = jnp.where(at == 0, 4e-7, 0.0)
        work[:, :n] = gram + identity * (jnp.sum(gram * identity) * shift)
        work[:, n:] = identity
        inverse_factor(work, n)
        v = mm(z, work[:, n:], 1, 1)
        found[...] = v
        moved[...] = mm(hn, v, 1, 0)
        return carry

    lax.fori_loop(0, 2, turn, 0)
    return found[...]


def first_kernel(g_ref, out_ref, work, moved, found):
    h = joined_gram(g_ref[:RANK], g_ref[RANK : 2 * RANK], g_ref[2 * RANK :])
    w = h.shape[0]
    v = vectors_of(h, work, moved, found)
    out_ref[:w] = v
    out_ref[w:] = mm(v, mm(h, v, 1, 0), 0, 0)


def scratch():
    return [
        pltpu.VMEM((RANK, 2 * RANK), F32),
        pltpu.VMEM((2 * RANK, RANK), F32),
        pltpu.VMEM((2 * RANK, RANK), F32),
    ]


def first_level(gram):
    return pl.pallas_call(
        first_kernel,
        out_shape=jax.ShapeDtypeStruct((3 * RANK, RANK), F32),
        scratch_shapes=scratch(),
    )(gram)


def joined_gram(own_gram, cross, far_gram):
    top = jnp.concatenate([own_gram, cross], axis=1)
    low = jnp.concatenate([cross.T, far_gram], axis=1)
    return jnp.concatenate([top, low], axis=0)


def level_kernel(own_ref, cross_ref, far_ref, out_ref, work, moved, found):
    w = own_ref.shape[0] - RANK
    h = joined_gram(own_ref[w:], cross_ref[...], far_ref[w:])
    u = vectors_of(h, work, moved, found)
    out_ref[:w] = mm(own_ref[:w], u[:RANK], 1, 0)
    out_ref[w : 2 * w] = mm(far_ref[:w], u[RANK:], 1, 0)
    out_ref[2 * w :] = mm(u, mm(h, u, 1, 0), 0, 0)


def next_level(own, cross, far):
    w = own.shape[0] - RANK
    return pl.pallas_call(
        level_kernel,
        out_shape=jax.ShapeDtypeStruct((2 * w + RANK, RANK), F32),
        scratch_shapes=scratch(),
    )(own, cross, far)


def last_kernel(own_ref, cross_ref, far_ref, pick_ref, out_ref, work, moved, found):
    w = own_ref.shape[0] - RANK
    h = joined_gram(own_ref[w:], cross_ref[...], far_ref[w:])
    u = vectors_of(h, work, moved, found)
    share = pick_ref.shape[0]
    for at, ref in ((0, own_ref), (1, far_ref)):
        mine = mm(pick_ref[...], u[at * RANK : (at + 1) * RANK], 1, 1)
        part = mm(mine, ref[:w], 1, 1)
        top = part.astype(BF)
        out_ref[:share, at * w : (at + 1) * w] = top
        out_ref[share:, at * w : (at + 1) * w] = (part - top.astype(F32)).astype(BF)


def last_level(own, cross, far, pick):
    w = own.shape[0] - RANK
    return pl.pallas_call(
        last_kernel,
        out_shape=jax.ShapeDtypeStruct((2 * pick.shape[0], 2 * w), BF),
        scratch_shapes=scratch(),
    )(own, cross, far, pick)


def project_kernel(own_ref, far_ref, *refs):
    *blocks, o_ref = refs
    w = own_ref.shape[0] - RANK
    own = own_ref[:w]
    total = jnp.zeros(o_ref.shape, F32)
    for g, block in enumerate(blocks):
        snaps = block.shape[0]
        seen = mm(block[...], own, 1, 0)
        total += mm(seen, far_ref[g * snaps : (g + 1) * snaps], 0, 0)
    o_ref[...] = total


def project(own, far, blocks):
    return pl.pallas_call(project_kernel, out_shape=jax.ShapeDtypeStruct((RANK, RANK), F32))(
        own, far, *blocks
    )


def feature_kernel(count, u_ref, halo_ref, *refs):
    left = refs[: 2 * count]
    hi_ref, lo_ref, gram_ref, field, sides, sums = refs[2 * count :]
    at = pl.program_id(0)
    _, height, wide, snaps = u_ref.shape

    def place(c, line, row):
        for h in range(snaps // 128):
            field[c, line, h, PAD : PAD + wide, :] = row[:, h * 128 : (h + 1) * 128]

    @pl.when(at == 0)
    def _():
        sides[...] = halo_ref[:, :, wide:, :].astype(F32)
        for c in range(2):
            place(c, 0, halo_ref[c, 0, :wide, :].astype(F32))
            place(c, height + 1, halo_ref[c, 1, :wide, :].astype(F32))
            place(c, 1, u_ref[c, 0].astype(F32))
        sums[...] = jnp.zeros_like(sums)

    def one(r, carry):
        i = at * ROWS + r

        @pl.when(i + 1 < height)
        def _():
            for c in range(2):
                place(c, i + 2, u_ref[c, i + 1].astype(F32))

        for c in range(2):
            for k, spot in ((0, PAD - 1), (1, PAD + wide)):
                row = sides[c, k, pl.ds(i, 1), :]
                for h in range(snaps // 128):
                    field[c, i + 1, h, spot : spot + 1, :] = row[:, h * 128 : (h + 1) * 128]

        for h in range(snaps // 128):

            def along_x(c):
                return (
                    field[c, i + 2, h, PAD : PAD + wide, :] - field[c, i, h, PAD : PAD + wide, :]
                )

            def along_y(c):
                return (
                    field[c, i + 1, h, PAD + 1 : PAD + 1 + wide, :]
                    - field[c, i + 1, h, PAD - 1 : PAD - 1 + wide, :]
                )

            strain_xx = along_x(0)
            strain_yy = along_y(1)
            shear = along_x(1) + along_y(0)
            values = (
                0.5 * (strain_xx + strain_yy),
                0.25 * (strain_xx * strain_yy) - 0.0625 * (shear * shear),
            )
            span = pl.ds(pl.multiple_of(r * wide, wide), wide)
            for k, value in enumerate(values):
                hi = value.astype(BF)
                hi_ref[k, span, h * 128 : (h + 1) * 128] = hi
                lo_ref[k, span, h * 128 : (h + 1) * 128] = (value - hi.astype(F32)).astype(BF)
        return carry

    lax.fori_loop(0, ROWS, one, 0)
    for k in range(2):
        hi = hi_ref[k]
        lo = lo_ref[k]
        if count == 0:
            sums[:, :snaps] += fast(hi, hi, 0, 0)
            sums[:, snaps:] += fast(hi, lo, 0, 0)
        for g in range(count):
            other = left[2 * g][k]
            rest = left[2 * g + 1][k]
            sums[:, g * snaps : (g + 1) * snaps] += (
                fast(hi, other, 0, 0) + fast(hi, rest, 0, 0) + fast(lo, other, 0, 0)
            )

    @pl.when(at == pl.num_programs(0) - 1)
    def _():
        if count == 0:
            mixed = sums[:, snaps:]
            total = sums[:, :snaps] + (mixed + mixed.T)
            gram_ref[:RANK] = total[:RANK, :RANK]
            gram_ref[RANK : 2 * RANK] = total[:RANK, RANK:]
            gram_ref[2 * RANK :] = total[RANK:, RANK:]
        else:
            gram_ref[...] = sums[:, : count * snaps]


def features(u, halo, lefts):
    _, height, wide, snaps = u.shape
    count = len(lefts)
    full = lambda array: pl.BlockSpec(array.shape, lambda i: (0,) * array.ndim)
    part = pl.BlockSpec((2, ROWS * wide, snaps), lambda i: (0, i, 0))
    half = jax.ShapeDtypeStruct((2, height * wide, snaps), BF)
    shape = (snaps, count * snaps) if count else (3 * RANK, RANK)
    hi, lo, gram = pl.pallas_call(
        lambda *refs: feature_kernel(count, *refs),
        grid=(height // ROWS,),
        in_specs=[full(u), full(halo)] + [part] * (2 * count),
        out_specs=(part, part, pl.BlockSpec(shape, lambda i: (0, 0))),
        out_shape=(half, half, jax.ShapeDtypeStruct(shape, F32)),
        scratch_shapes=[
            pltpu.VMEM((2, height + 2, snaps // 128, wide + 2 * PAD, 128), F32),
            pltpu.VMEM((2, 2, height, snaps), F32),
            pltpu.VMEM((snaps, max(count, 2) * snaps), F32),
        ],
        compiler_params=pltpu.CompilerParams(vmem_limit_bytes=LIMIT),
    )(u, halo, *[array for pair in lefts for array in pair])
    return (hi, lo), gram


def finish_kernel(*refs):
    *halves, w_ref, o_ref = refs
    groups = len(halves) // 2
    snaps = w_ref.shape[1] // groups
    share = w_ref.shape[0] // 2
    wide = o_ref.shape[-1]
    total = jnp.zeros((share, halves[0].shape[1]), F32)
    for g in range(groups):
        w = w_ref[:, g * snaps : (g + 1) * snaps]
        both = fast(w, halves[2 * g][0], 1, 1)
        total += both[:share] + both[share:]
        total += fast(w[:share], halves[2 * g + 1][0], 1, 1)
    for r in range(o_ref.shape[1]):
        o_ref[0, r] = total[:, r * wide : (r + 1) * wide]


def finish(pairs, weights, height, wide):
    rows = 8
    _, _, snaps = pairs[0][0].shape
    share = weights.shape[0] // 2
    part = pl.BlockSpec((1, rows * wide, snaps), lambda k, i: (k, i, 0))
    return pl.pallas_call(
        finish_kernel,
        grid=(2, height // rows),
        in_specs=[part] * (2 * len(pairs))
        + [pl.BlockSpec(weights.shape, lambda k, i: (0, 0))],
        out_specs=pl.BlockSpec((1, rows, share, wide), lambda k, i: (k, i, 0, 0)),
        out_shape=jax.ShapeDtypeStruct((2, height, share, wide), F32),
        compiler_params=pltpu.CompilerParams(vmem_limit_bytes=LIMIT),
    )(*[array for pair in pairs for array in pair], weights)


def edges(block, axis, dim):
    count = lax.axis_size(axis)
    forward = [(i, i + 1) for i in range(count - 1)]
    backward = [(target, source) for source, target in forward]
    low = lax.ppermute(
        lax.slice_in_dim(block, block.shape[dim] - 1, None, axis=dim), axis, forward
    )
    high = lax.ppermute(lax.slice_in_dim(block, 0, 1, axis=dim), axis, backward)
    return low, high


def halo_of(block):
    x_low, x_high = edges(block, "gx", 1)
    y_low, y_high = edges(block, "gy", 2)
    low = jnp.concatenate([x_low[:, 0], y_low[:, :, 0]], axis=1)
    high = jnp.concatenate([x_high[:, 0], y_high[:, :, 0]], axis=1)
    return jnp.stack([low, high], axis=1)


def swapped(value, mask):
    pairs = [(source, source ^ mask) for source in range(lax.axis_size("cyc"))]
    return lax.ppermute(value, "cyc", pairs)


def scatter_sum(value, axis):
    count = lax.axis_size(axis)
    parts = lax.all_to_all(value, axis, 0, 0, tiled=True)
    return parts.reshape(count, -1, value.shape[1]).sum(0)


def gathered(value, axis):
    count = lax.axis_size(axis)
    copies = jnp.broadcast_to(value[None], (count,) + value.shape)
    return lax.all_to_all(copies.reshape(-1, value.shape[1]), axis, 0, 0, tiled=True)


def all_sum(value):
    flat = value.reshape(-1, 128)
    part = scatter_sum(flat, "gx")
    part = gathered(part, "gy")
    part = part.reshape(lax.axis_size("gy"), -1, 128).sum(0)
    return gathered(part, "gx").reshape(value.shape)


def whole(displacement):
    _, height, wide, _ = displacement.shape
    groups = lax.axis_size("cyc")
    halo = halo_of(displacement)
    near = swapped(displacement, 1)
    side = swapped(displacement, 3)
    near_halo, far_halo, side_halo = (swapped(halo, mask) for mask in (1, 2, 3))
    own, gram = features(displacement, halo, [])
    total = all_sum(gram)
    level0 = first_level(total)
    other0 = swapped(level0, 1)
    relayed, _ = lax.optimization_barrier((near, total))
    far = swapped(relayed, 3)
    pair, cross1 = features(near, near_halo, [own])
    total = all_sum(project(level0, other0, [cross1]))
    level1 = next_level(level0, total, other0)
    other1 = swapped(level1, 2)
    fourth, cross3 = features(side, side_halo, [own, pair])
    third, cross2 = features(far, far_halo, [own, pair])
    share = RANK // groups
    column = lax.axis_index("cyc") * share + jnp.arange(share)
    pick = (column[:, None] == jnp.arange(RANK)[None, :]).astype(F32)
    total = all_sum(project(level1, other1, [cross2, cross3]))
    weights = last_level(level1, total, other1, pick)
    result = finish([own, pair, third, fourth], weights, height, wide)
    return result.transpose(0, 1, 3, 2)


def solution(mesh):
    return jax.shard_map(
        whole,
        mesh=mesh,
        in_specs=(P(None, "gx", "gy", "cyc"),),
        out_specs=P(None, "gx", "gy", "cyc"),
        check_vma=False,
    )
```

```python
import jax
import jax.numpy as jnp
from jax import lax
from jax.experimental import pallas as pl
from jax.experimental.pallas import tpu as pltpu
from jax.sharding import PartitionSpec as P

RANK = 128
F32 = jnp.float32
BF = jnp.bfloat16
HIGH = lax.Precision.HIGHEST
ROWS = 4
PAD = 8
LIMIT = 56 * 2**20


def mm(a, b, ca, cb):
    return lax.dot_general(
        a, b, (((ca,), (cb,)), ((), ())), precision=HIGH, preferred_element_type=F32
    )


def fast(a, b, ca, cb):
    return lax.dot_general(a, b, (((ca,), (cb,)), ((), ())), preferred_element_type=F32)


def thirds(v):
    top = v.astype(BF).astype(F32)
    rest = v - top
    mid = rest.astype(BF).astype(F32)
    return top, mid, rest - mid


def small_inverse(entry, n):
    d = [row[:] for row in entry]
    l = [[None] * n for _ in range(n)]
    r = [None] * n
    for j in range(n):
        g = lax.rsqrt(d[j][j])
        g = g * (1.5 - (0.5 * d[j][j]) * (g * g))
        r[j] = g
        for i in range(j + 1, n):
            l[i][j] = d[i][j] * g
        for k in range(j + 1, n):
            for i in range(k, n):
                d[i][k] = d[i][k] - l[i][j] * l[k][j]
    x = [[None] * n for _ in range(n)]
    for j in range(n):
        x[j][j] = r[j]
        for i in range(j + 1, n):
            t = l[i][j] * x[j][j]
            for k in range(j + 1, i):
                t = t + l[i][k] * x[k][j]
            x[i][j] = -(t * r[i])
    return x


def inverse_factor(work, n):
    step = 8
    sub = lax.broadcasted_iota(jnp.int32, (step, n), 0)
    for at in range(0, n, step):
        rows = work[at : at + step, :]
        block = rows[:, at : at + step]
        entry = [
            [jnp.broadcast_to(block[i : i + 1, j : j + 1], (step, n)) for j in range(i + 1)]
            for i in range(step)
        ]
        x = small_inverse(entry, step)
        left = jnp.zeros((step, n), F32)
        right = jnp.zeros((step, n), F32)
        for j in range(step):
            col = x[j][j]
            for i in range(j + 1, step):
                col = jnp.where(sub >= i, x[i][j], col)
            col = jnp.where(sub < j, 0.0, col)
            left = left + col * jnp.broadcast_to(rows[j : j + 1, :n], (step, n))
            right = right + col * jnp.broadcast_to(rows[j : j + 1, n:], (step, n))
        new = jnp.concatenate([left, right], axis=1)
        work[at : at + step, :] = new
        if at + step < n:
            a, b, c = thirds(new)
            lhs = jnp.concatenate([a, a, a, b, b, c], axis=0)[:, :n].astype(BF)
            rhs = jnp.concatenate([a, b, c, a, b, a], axis=0).astype(BF)
            prod = fast(lhs, rhs, 0, 0)
            work[at + step :, :] = work[at + step :, :] - prod[at + step :, :]


def eye(n):
    row = lax.broadcasted_iota(jnp.int32, (n, n), 0)
    return (row == lax.broadcasted_iota(jnp.int32, (n, n), 1)).astype(F32)


def vectors_of(h, work, moved, found):
    w = h.shape[0]
    n = w // 2
    identity = eye(n)
    trace = jnp.sum(h[:n, :n] * identity) + jnp.sum(h[n:, n:] * identity)
    hn = h * (1.0 / (trace / w + 1e-06))
    moved[...] = mm(hn, hn[:, :n] + hn[:, n:], 1, 0)

    def turn(at, carry):
        z = moved[...]
        gram = mm(z, z, 0, 0)
        shift = jnp.where(at == 0, 4e-7, 0.0)
        work[:, :n] = gram + identity * (jnp.sum(gram * identity) * shift)
        work[:, n:] = identity
        inverse_factor(work, n)
        v = mm(z, work[:, n:], 1, 1)
        found[...] = v
        moved[...] = mm(hn, v, 1, 0)
        return carry

    lax.fori_loop(0, 2, turn, 0)
    return found[...]


def first_kernel(g_ref, out_ref, work, moved, found):
    h = joined_gram(g_ref[:RANK], g_ref[RANK : 2 * RANK], g_ref[2 * RANK :])
    w = h.shape[0]
    v = vectors_of(h, work, moved, found)
    out_ref[:w] = v
    out_ref[w:] = mm(v, mm(h, v, 1, 0), 0, 0)


def scratch():
    return [
        pltpu.VMEM((RANK, 2 * RANK), F32),
        pltpu.VMEM((2 * RANK, RANK), F32),
        pltpu.VMEM((2 * RANK, RANK), F32),
    ]


def first_level(gram):
    return pl.pallas_call(
        first_kernel,
        out_shape=jax.ShapeDtypeStruct((3 * RANK, RANK), F32),
        scratch_shapes=scratch(),
    )(gram)


def joined_gram(own_gram, cross, far_gram):
    top = jnp.concatenate([own_gram, cross], axis=1)
    low = jnp.concatenate([cross.T, far_gram], axis=1)
    return jnp.concatenate([top, low], axis=0)


def level_kernel(own_ref, cross_ref, far_ref, out_ref, work, moved, found):
    w = own_ref.shape[0] - RANK
    h = joined_gram(own_ref[w:], cross_ref[...], far_ref[w:])
    u = vectors_of(h, work, moved, found)
    out_ref[:w] = mm(own_ref[:w], u[:RANK], 1, 0)
    out_ref[w : 2 * w] = mm(far_ref[:w], u[RANK:], 1, 0)
    out_ref[2 * w :] = mm(u, mm(h, u, 1, 0), 0, 0)


def next_level(own, cross, far):
    w = own.shape[0] - RANK
    return pl.pallas_call(
        level_kernel,
        out_shape=jax.ShapeDtypeStruct((2 * w + RANK, RANK), F32),
        scratch_shapes=scratch(),
    )(own, cross, far)


def last_kernel(own_ref, cross_ref, far_ref, pick_ref, out_ref, work, moved, found):
    w = own_ref.shape[0] - RANK
    h = joined_gram(own_ref[w:], cross_ref[...], far_ref[w:])
    u = vectors_of(h, work, moved, found)
    share = pick_ref.shape[0]
    part = mm(pick_ref[...], u, 1, 1)
    top = part.astype(BF)
    out_ref[:share] = top
    out_ref[share:] = (part - top.astype(F32)).astype(BF)


def last_level(own, cross, far, pick):
    return pl.pallas_call(
        last_kernel,
        out_shape=jax.ShapeDtypeStruct((2 * pick.shape[0], 2 * RANK), BF),
        scratch_shapes=scratch(),
    )(own, cross, far, pick)


def project_kernel(own_ref, far_ref, *refs):
    *blocks, o_ref = refs
    w = own_ref.shape[0] - RANK
    own = own_ref[:w]
    total = jnp.zeros(o_ref.shape, F32)
    for g, block in enumerate(blocks):
        snaps = block.shape[0]
        seen = mm(block[...], own, 1, 0)
        total += mm(seen, far_ref[g * snaps : (g + 1) * snaps], 0, 0)
    o_ref[...] = total


def project(own, far, blocks):
    return pl.pallas_call(
        project_kernel,
        out_shape=jax.ShapeDtypeStruct((RANK, RANK), F32),
    )(own, far, *blocks)


def feature_kernel(count, height, first_ref, u_ref, halo_ref, *refs):
    left = refs[: 2 * count]
    hi_ref, lo_ref, gram_ref, field, sides, sums = refs[2 * count :]
    at = pl.program_id(0)
    _, _, wide, snaps = u_ref.shape

    def place(c, line, row):
        for h in range(snaps // 128):
            field[c, line, h, PAD : PAD + wide, :] = row[:, h * 128 : (h + 1) * 128]

    @pl.when(at == 0)
    def _():
        sides[...] = halo_ref[:, :, wide:, :].astype(F32)
        for c in range(2):
            place(c, 0, halo_ref[c, 0, :wide, :].astype(F32))
            place(c, height + 1, halo_ref[c, 1, :wide, :].astype(F32))
            for r in range(ROWS):
                place(c, 1 + r, first_ref[c, r].astype(F32))
        sums[...] = jnp.zeros_like(sums)

    @pl.when((at + 1) * ROWS < height)
    def _():
        for c in range(2):
            place(c, (at + 1) * ROWS + 1, u_ref[c, 0].astype(F32))

    def one(r, carry):
        i = at * ROWS + r

        @pl.when((r > 0) & (i + ROWS < height))
        def _():
            for c in range(2):
                place(c, i + ROWS + 1, u_ref[c, r].astype(F32))

        for c in range(2):
            for k, spot in ((0, PAD - 1), (1, PAD + wide)):
                row = sides[c, k, pl.ds(i, 1), :]
                for h in range(snaps // 128):
                    field[c, i + 1, h, spot : spot + 1, :] = row[:, h * 128 : (h + 1) * 128]

        for h in range(snaps // 128):

            def along_x(c):
                return (
                    field[c, i + 2, h, PAD : PAD + wide, :] - field[c, i, h, PAD : PAD + wide, :]
                )

            def along_y(c):
                return (
                    field[c, i + 1, h, PAD + 1 : PAD + 1 + wide, :]
                    - field[c, i + 1, h, PAD - 1 : PAD - 1 + wide, :]
                )

            strain_xx = along_x(0)
            strain_yy = along_y(1)
            shear = along_x(1) + along_y(0)
            values = (
                0.5 * (strain_xx + strain_yy),
                0.25 * (strain_xx * strain_yy) - 0.0625 * (shear * shear),
            )
            span = pl.ds(pl.multiple_of(r * wide, wide), wide)
            for k, value in enumerate(values):
                hi = value.astype(BF)
                hi_ref[k, span, h * 128 : (h + 1) * 128] = hi
                lo_ref[k, span, h * 128 : (h + 1) * 128] = (value - hi.astype(F32)).astype(BF)
        return carry

    lax.fori_loop(0, ROWS, one, 0)
    for k in range(2):
        hi = hi_ref[k]
        lo = lo_ref[k]
        if count == 0:
            sums[:, :snaps] += fast(hi, hi, 0, 0)
            sums[:, snaps:] += fast(hi, lo, 0, 0)
        for g in range(count):
            other = left[2 * g][k]
            rest = left[2 * g + 1][k]
            sums[:, g * snaps : (g + 1) * snaps] += (
                fast(hi, other, 0, 0) + fast(hi, rest, 0, 0) + fast(lo, other, 0, 0)
            )

    @pl.when(at == pl.num_programs(0) - 1)
    def _():
        if count == 0:
            mixed = sums[:, snaps:]
            total = sums[:, :snaps] + (mixed + mixed.T)
            gram_ref[:RANK] = total[:RANK, :RANK]
            gram_ref[RANK : 2 * RANK] = total[:RANK, RANK:]
            gram_ref[2 * RANK :] = total[RANK:, RANK:]
        else:
            gram_ref[...] = sums[:, : count * snaps]


def features(u, halo, lefts):
    _, height, wide, snaps = u.shape
    count = len(lefts)
    last = height // ROWS - 1
    full = lambda array: pl.BlockSpec(array.shape, lambda i: (0,) * array.ndim)
    part = pl.BlockSpec((2, ROWS * wide, snaps), lambda i: (0, i, 0))
    half = jax.ShapeDtypeStruct((2, height * wide, snaps), BF)
    shape = (snaps, count * snaps) if count else (3 * RANK, RANK)
    hi, lo, gram = pl.pallas_call(
        lambda *refs: feature_kernel(count, height, *refs),
        grid=(height // ROWS,),
        in_specs=[
            pl.BlockSpec((2, ROWS, wide, snaps), lambda i: (0, 0, 0, 0)),
            pl.BlockSpec((2, ROWS, wide, snaps), lambda i: (0, jnp.minimum(i + 1, last), 0, 0)),
            full(halo),
        ]
        + [part] * (2 * count),
        out_specs=(part, part, pl.BlockSpec(shape, lambda i: (0, 0))),
        out_shape=(half, half, jax.ShapeDtypeStruct(shape, F32)),
        scratch_shapes=[
            pltpu.VMEM((2, height + 2, snaps // 128, wide + 2 * PAD, 128), F32),
            pltpu.VMEM((2, 2, height, snaps), F32),
            pltpu.VMEM((snaps, max(count, 2) * snaps), F32),
        ],
        compiler_params=pltpu.CompilerParams(vmem_limit_bytes=LIMIT),
    )(u, u, halo, *[array for pair in lefts for array in pair])
    return (hi, lo), gram


def mix_kernel(*refs):
    *halves, w_ref, o_ref = refs
    groups = len(halves) // 2
    snaps = halves[0].shape[2]
    total = jnp.zeros(o_ref.shape[1:], F32)
    for g in range(groups):
        w = w_ref[g * snaps : (g + 1) * snaps]
        top = w.astype(BF)
        low = (w - top.astype(F32)).astype(BF)
        hi = halves[2 * g][0]
        both = fast(hi, jnp.concatenate([top, low], axis=1), 1, 0)
        total += both[:, :RANK] + both[:, RANK:]
        total += fast(halves[2 * g + 1][0], top, 1, 0)
    o_ref[0] = total


def mix(pairs, vectors):
    chunk = 1024
    _, nodes, snaps = pairs[0][0].shape
    part = pl.BlockSpec((1, chunk, snaps), lambda k, i: (k, i, 0))
    return pl.pallas_call(
        mix_kernel,
        grid=(2, nodes // chunk),
        in_specs=[part] * (2 * len(pairs))
        + [pl.BlockSpec(vectors.shape, lambda k, i: (0, 0))],
        out_specs=pl.BlockSpec((1, chunk, RANK), lambda k, i: (k, i, 0)),
        out_shape=jax.ShapeDtypeStruct((2, nodes, RANK), F32),
        compiler_params=pltpu.CompilerParams(vmem_limit_bytes=LIMIT),
    )(*[array for pair in pairs for array in pair], vectors)


def finish_kernel(first_ref, second_ref, w_ref, o_ref):
    share = w_ref.shape[0] // 2
    wide = o_ref.shape[-1]
    total = jnp.zeros((share, first_ref.shape[1]), F32)
    for g, ref in enumerate((first_ref, second_ref)):
        w = w_ref[:, g * RANK : (g + 1) * RANK]
        value = ref[0]
        hi = value.astype(BF)
        lo = (value - hi.astype(F32)).astype(BF)
        both = fast(w, hi, 1, 1)
        total += both[:share] + both[share:]
        total += fast(w[:share], lo, 1, 1)
    for r in range(o_ref.shape[1]):
        o_ref[0, r] = total[:, r * wide : (r + 1) * wide]


def finish(first, second, weights, height, wide):
    rows = 8
    share = weights.shape[0] // 2
    part = pl.BlockSpec((1, rows * wide, RANK), lambda k, i: (k, i, 0))
    return pl.pallas_call(
        finish_kernel,
        grid=(2, height // rows),
        in_specs=[part, part, pl.BlockSpec(weights.shape, lambda k, i: (0, 0))],
        out_specs=pl.BlockSpec((1, rows, share, wide), lambda k, i: (k, i, 0, 0)),
        out_shape=jax.ShapeDtypeStruct((2, height, share, wide), F32),
        compiler_params=pltpu.CompilerParams(vmem_limit_bytes=LIMIT),
    )(first, second, weights)


def edges(block, axis, dim):
    count = lax.axis_size(axis)
    forward = [(i, i + 1) for i in range(count - 1)]
    backward = [(target, source) for source, target in forward]
    low = lax.ppermute(
        lax.slice_in_dim(block, block.shape[dim] - 1, None, axis=dim), axis, forward
    )
    high = lax.ppermute(lax.slice_in_dim(block, 0, 1, axis=dim), axis, backward)
    return low, high


def halo_of(block):
    x_low, x_high = edges(block, "gx", 1)
    y_low, y_high = edges(block, "gy", 2)
    low = jnp.concatenate([x_low[:, 0], y_low[:, :, 0]], axis=1)
    high = jnp.concatenate([x_high[:, 0], y_high[:, :, 0]], axis=1)
    return jnp.stack([low, high], axis=1)


def swapped(value, mask):
    pairs = [(source, source ^ mask) for source in range(lax.axis_size("cyc"))]
    return lax.ppermute(value, "cyc", pairs)


def scatter_sum(value, axis):
    count = lax.axis_size(axis)
    parts = lax.all_to_all(value, axis, 0, 0, tiled=True)
    return parts.reshape(count, -1, value.shape[1]).sum(0)


def gathered(value, axis):
    count = lax.axis_size(axis)
    copies = jnp.broadcast_to(value[None], (count,) + value.shape)
    return lax.all_to_all(copies.reshape(-1, value.shape[1]), axis, 0, 0, tiled=True)


def all_sum(value):
    flat = value.reshape(-1, 128)
    part = scatter_sum(flat, "gx")
    part = gathered(part, "gy")
    part = part.reshape(lax.axis_size("gy"), -1, 128).sum(0)
    return gathered(part, "gx").reshape(value.shape)


def whole(displacement):
    _, height, wide, _ = displacement.shape
    groups = lax.axis_size("cyc")
    halo = halo_of(displacement)
    near = swapped(displacement, 1)
    side = swapped(displacement, 3)
    near_halo, far_halo, side_halo = (swapped(halo, mask) for mask in (1, 2, 3))
    own, gram = features(displacement, halo, [])
    total = all_sum(gram)
    level0 = first_level(total)
    other0 = swapped(level0, 1)
    relayed, _ = lax.optimization_barrier((near, total))
    far = swapped(relayed, 3)
    pair, cross1 = features(near, near_halo, [own])
    total = all_sum(project(level0, other0, [cross1]))
    level1 = next_level(level0, total, other0)
    other1 = swapped(level1, 2)
    fourth, cross3 = features(side, side_halo, [own, pair])
    third, cross2 = features(far, far_halo, [own, pair])
    share = RANK // groups
    column = lax.axis_index("cyc") * share + jnp.arange(share)
    pick = (column[:, None] == jnp.arange(RANK)[None, :]).astype(F32)
    total = all_sum(project(level1, other1, [cross2, cross3]))
    first = mix([own, pair], level1[: 4 * RANK])
    second = mix([third, fourth], other1[: 4 * RANK])
    weights = last_level(level1, total, other1, pick)
    result = finish(first, second, weights, height, wide)
    return result.transpose(0, 1, 3, 2)


def solution(mesh):
    return jax.shard_map(
        whole,
        mesh=mesh,
        in_specs=(P(None, "gx", "gy", "cyc"),),
        out_specs=P(None, "gx", "gy", "cyc"),
        check_vma=False,
    )
```

```python
import jax
import jax.numpy as jnp
from jax import lax
from jax.experimental import pallas as pl
from jax.experimental.pallas import tpu as pltpu
from jax.sharding import PartitionSpec as P

RANK = 128
F32 = jnp.float32
BF = jnp.bfloat16
HIGH = lax.Precision.HIGHEST
ROWS = 8
PAD = 8
LIMIT = 56 * 2**20


def mm(a, b, ca, cb):
    return lax.dot_general(
        a, b, (((ca,), (cb,)), ((), ())), precision=HIGH, preferred_element_type=F32
    )


def fast(a, b, ca, cb):
    return lax.dot_general(a, b, (((ca,), (cb,)), ((), ())), preferred_element_type=F32)


def thirds(v):
    top = v.astype(BF).astype(F32)
    rest = v - top
    mid = rest.astype(BF).astype(F32)
    return top, mid, rest - mid


def small_inverse(entry, n):
    d = [row[:] for row in entry]
    l = [[None] * n for _ in range(n)]
    r = [None] * n
    for j in range(n):
        g = lax.rsqrt(d[j][j])
        g = g * (1.5 - (0.5 * d[j][j]) * (g * g))
        r[j] = g
        for i in range(j + 1, n):
            l[i][j] = d[i][j] * g
        for k in range(j + 1, n):
            for i in range(k, n):
                d[i][k] = d[i][k] - l[i][j] * l[k][j]
    x = [[None] * n for _ in range(n)]
    for j in range(n):
        x[j][j] = r[j]
        for i in range(j + 1, n):
            t = l[i][j] * x[j][j]
            for k in range(j + 1, i):
                t = t + l[i][k] * x[k][j]
            x[i][j] = -(t * r[i])
    return x


def inverse_factor(work, n):
    step = 8
    sub = lax.broadcasted_iota(jnp.int32, (step, n), 0)
    for at in range(0, n, step):
        rows = work[at : at + step, :]
        block = rows[:, at : at + step]
        entry = [
            [jnp.broadcast_to(block[i : i + 1, j : j + 1], (step, n)) for j in range(i + 1)]
            for i in range(step)
        ]
        x = small_inverse(entry, step)
        left = jnp.zeros((step, n), F32)
        right = jnp.zeros((step, n), F32)
        for j in range(step):
            col = x[j][j]
            for i in range(j + 1, step):
                col = jnp.where(sub >= i, x[i][j], col)
            col = jnp.where(sub < j, 0.0, col)
            left = left + col * jnp.broadcast_to(rows[j : j + 1, :n], (step, n))
            right = right + col * jnp.broadcast_to(rows[j : j + 1, n:], (step, n))
        new = jnp.concatenate([left, right], axis=1)
        work[at : at + step, :] = new
        if at + step < n:
            a, b, c = thirds(new)
            lhs = jnp.concatenate([a, a, a, b, b, c], axis=0)[:, :n].astype(BF)
            rhs = jnp.concatenate([a, b, c, a, b, a], axis=0).astype(BF)
            prod = fast(lhs, rhs, 0, 0)
            work[at + step :, :] = work[at + step :, :] - prod[at + step :, :]


def halves(v):
    top = v.astype(BF)
    return top, (v - top.astype(F32)).astype(BF)


def split_mm(a, b, ca, cb):
    a0, a1 = halves(a)
    b0, b1 = halves(b)
    return fast(a0, b0, ca, cb) + (fast(a0, b1, ca, cb) + fast(a1, b0, ca, cb))


def eye(n):
    row = lax.broadcasted_iota(jnp.int32, (n, n), 0)
    return (row == lax.broadcasted_iota(jnp.int32, (n, n), 1)).astype(F32)


def vectors_of(h, work, moved, found, last=False):
    w = h.shape[0]
    n = w // 2
    identity = eye(n)
    trace = jnp.sum(h[:n, :n] * identity) + jnp.sum(h[n:, n:] * identity)
    level = trace / w + 1e-06
    hn = h * (1.0 / level)
    moved[...] = mm(hn, hn[:, :n] + hn[:, n:], 1, 0)

    def turn(at, carry):
        z = moved[...]
        gram = mm(z, z, 0, 0)
        shift = jnp.where(at == 0, 4e-7, 0.0)
        work[:, :n] = gram + identity * (jnp.sum(gram * identity) * shift)
        work[:, n:] = identity
        inverse_factor(work, n)
        v = mm(z, work[:, n:], 1, 1)
        found[...] = v
        if last:

            @pl.when(at == 0)
            def _():
                moved[...] = mm(hn, v, 1, 0)

        else:
            moved[...] = mm(hn, v, 1, 0)
        return carry

    lax.fori_loop(0, 2, turn, 0)
    v = found[...]
    if last:
        return v, None
    return v, mm(v, moved[...], 0, 0) * level


def first_kernel(g_ref, out_ref, work, moved, found):
    h = joined_gram(g_ref[:RANK], g_ref[RANK : 2 * RANK], g_ref[2 * RANK :])
    w = h.shape[0]
    v, gram = vectors_of(h, work, moved, found)
    out_ref[:w] = v
    out_ref[w:] = gram


def scratch():
    return [
        pltpu.VMEM((RANK, 2 * RANK), F32),
        pltpu.VMEM((2 * RANK, RANK), F32),
        pltpu.VMEM((2 * RANK, RANK), F32),
    ]


def first_level(gram):
    return pl.pallas_call(
        first_kernel,
        out_shape=jax.ShapeDtypeStruct((3 * RANK, RANK), F32),
        scratch_shapes=scratch(),
    )(gram)


def joined_gram(own_gram, cross, far_gram):
    top = jnp.concatenate([own_gram, cross], axis=1)
    low = jnp.concatenate([cross.T, far_gram], axis=1)
    return jnp.concatenate([top, low], axis=0)


def level_kernel(own_ref, cross_ref, far_ref, out_ref, work, moved, found):
    w = own_ref.shape[0] - RANK
    h = joined_gram(own_ref[w:], cross_ref[...], far_ref[w:])
    u, gram = vectors_of(h, work, moved, found)
    out_ref[:w] = mm(own_ref[:w], u[:RANK], 1, 0)
    out_ref[w : 2 * w] = mm(far_ref[:w], u[RANK:], 1, 0)
    out_ref[2 * w :] = gram


def next_level(own, cross, far):
    w = own.shape[0] - RANK
    return pl.pallas_call(
        level_kernel,
        out_shape=jax.ShapeDtypeStruct((2 * w + RANK, RANK), F32),
        scratch_shapes=scratch(),
    )(own, cross, far)


def last_kernel(own_ref, cross_ref, far_ref, pick_ref, out_ref, work, moved, found):
    w = own_ref.shape[0] - RANK
    h = joined_gram(own_ref[w:], cross_ref[...], far_ref[w:])
    u, _ = vectors_of(h, work, moved, found, last=True)
    share = pick_ref.shape[0]
    for at, ref in ((0, own_ref), (1, far_ref)):
        mine = mm(pick_ref[...], u[at * RANK : (at + 1) * RANK], 1, 1)
        part = mm(mine, ref[:w], 1, 1)
        top = part.astype(BF)
        out_ref[:share, at * w : (at + 1) * w] = top
        out_ref[share:, at * w : (at + 1) * w] = (part - top.astype(F32)).astype(BF)


def last_level(own, cross, far, pick):
    w = own.shape[0] - RANK
    return pl.pallas_call(
        last_kernel,
        out_shape=jax.ShapeDtypeStruct((2 * pick.shape[0], 2 * w), BF),
        scratch_shapes=scratch(),
    )(own, cross, far, pick)


def project_kernel(own_ref, far_ref, *refs):
    *blocks, o_ref = refs
    w = own_ref.shape[0] - RANK
    own = own_ref[:w]
    total = jnp.zeros(o_ref.shape, F32)
    for g, block in enumerate(blocks):
        snaps = block.shape[0]
        seen = split_mm(block[...], own, 1, 0)
        total += split_mm(seen, far_ref[g * snaps : (g + 1) * snaps], 0, 0)
    o_ref[...] = total


def project(own, far, blocks):
    return pl.pallas_call(
        project_kernel,
        out_shape=jax.ShapeDtypeStruct((RANK, RANK), F32),
    )(own, far, *blocks)


def feature_kernel(count, height, first_ref, u_ref, halo_ref, *refs):
    left = refs[: 2 * count]
    hi_ref, lo_ref, gram_ref, field, sides, sums = refs[2 * count :]
    at = pl.program_id(0)
    _, _, wide, snaps = u_ref.shape

    def place(c, line, row):
        for h in range(snaps // 128):
            field[c, line, h, PAD : PAD + wide, :] = row[:, h * 128 : (h + 1) * 128]

    @pl.when(at == 0)
    def _():
        sides[...] = halo_ref[:, :, wide:, :].astype(F32)
        for c in range(2):
            place(c, 0, halo_ref[c, 0, :wide, :].astype(F32))
            place(c, height + 1, halo_ref[c, 1, :wide, :].astype(F32))
            for r in range(ROWS):
                place(c, 1 + r, first_ref[c, r].astype(F32))
        sums[...] = jnp.zeros_like(sums)

    @pl.when((at + 1) * ROWS < height)
    def _():
        for c in range(2):
            place(c, (at + 1) * ROWS + 1, u_ref[c, 0].astype(F32))

    def one(r, carry):
        i = at * ROWS + r

        @pl.when((r > 0) & (i + ROWS < height))
        def _():
            for c in range(2):
                place(c, i + ROWS + 1, u_ref[c, r].astype(F32))

        for c in range(2):
            for k, spot in ((0, PAD - 1), (1, PAD + wide)):
                row = sides[c, k, pl.ds(i, 1), :]
                for h in range(snaps // 128):
                    field[c, i + 1, h, spot : spot + 1, :] = row[:, h * 128 : (h + 1) * 128]

        for h in range(snaps // 128):

            def along_x(c):
                return (
                    field[c, i + 2, h, PAD : PAD + wide, :] - field[c, i, h, PAD : PAD + wide, :]
                )

            def along_y(c):
                return (
                    field[c, i + 1, h, PAD + 1 : PAD + 1 + wide, :]
                    - field[c, i + 1, h, PAD - 1 : PAD - 1 + wide, :]
                )

            strain_xx = along_x(0)
            strain_yy = along_y(1)
            shear = along_x(1) + along_y(0)
            values = (
                0.5 * (strain_xx + strain_yy),
                0.25 * (strain_xx * strain_yy) - 0.0625 * (shear * shear),
            )
            span = pl.ds(pl.multiple_of(r * wide, wide), wide)
            for k, value in enumerate(values):
                hi = value.astype(BF)
                hi_ref[k, span, h * 128 : (h + 1) * 128] = hi
                lo_ref[k, span, h * 128 : (h + 1) * 128] = (value - hi.astype(F32)).astype(BF)
        return carry

    lax.fori_loop(0, ROWS, one, 0)
    for k in range(2):
        hi = hi_ref[k]
        lo = lo_ref[k]
        if count == 0:
            sums[:, :snaps] += fast(hi, hi, 0, 0)
            sums[:, snaps:] += fast(hi, lo, 0, 0)
        for g in range(count):
            other = left[2 * g][k]
            rest = left[2 * g + 1][k]
            sums[:, g * snaps : (g + 1) * snaps] += (
                fast(hi, other, 0, 0) + fast(hi, rest, 0, 0) + fast(lo, other, 0, 0)
            )

    @pl.when(at == pl.num_programs(0) - 1)
    def _():
        if count == 0:
            mixed = sums[:, snaps:]
            total = sums[:, :snaps] + (mixed + mixed.T)
            gram_ref[:RANK] = total[:RANK, :RANK]
            gram_ref[RANK : 2 * RANK] = total[:RANK, RANK:]
            gram_ref[2 * RANK :] = total[RANK:, RANK:]
        else:
            gram_ref[...] = sums[:, : count * snaps]


def features(u, halo, lefts):
    _, height, wide, snaps = u.shape
    count = len(lefts)
    last = height // ROWS - 1
    full = lambda array: pl.BlockSpec(array.shape, lambda i: (0,) * array.ndim)
    part = pl.BlockSpec((2, ROWS * wide, snaps), lambda i: (0, i, 0))
    half = jax.ShapeDtypeStruct((2, height * wide, snaps), BF)
    shape = (snaps, count * snaps) if count else (3 * RANK, RANK)
    hi, lo, gram = pl.pallas_call(
        lambda *refs: feature_kernel(count, height, *refs),
        grid=(height // ROWS,),
        in_specs=[
            pl.BlockSpec((2, ROWS, wide, snaps), lambda i: (0, 0, 0, 0)),
            pl.BlockSpec((2, ROWS, wide, snaps), lambda i: (0, jnp.minimum(i + 1, last), 0, 0)),
            full(halo),
        ]
        + [part] * (2 * count),
        out_specs=(part, part, pl.BlockSpec(shape, lambda i: (0, 0))),
        out_shape=(half, half, jax.ShapeDtypeStruct(shape, F32)),
        scratch_shapes=[
            pltpu.VMEM((2, height + 2, snaps // 128, wide + 2 * PAD, 128), F32),
            pltpu.VMEM((2, 2, height, snaps), F32),
            pltpu.VMEM((snaps, max(count, 2) * snaps), F32),
        ],
        compiler_params=pltpu.CompilerParams(vmem_limit_bytes=LIMIT),
    )(u, u, halo, *[array for pair in lefts for array in pair])
    return (hi, lo), gram


def finish_kernel(*refs):
    *halves, w_ref, o_ref = refs
    groups = len(halves) // 2
    snaps = w_ref.shape[1] // groups
    share = w_ref.shape[0] // 2
    wide = o_ref.shape[-1]
    total = jnp.zeros((share, halves[0].shape[1]), F32)
    for g in range(groups):
        w = w_ref[:, g * snaps : (g + 1) * snaps]
        both = fast(w, halves[2 * g][0], 1, 1)
        total += both[:share] + both[share:]
        total += fast(w[:share], halves[2 * g + 1][0], 1, 1)
    for r in range(o_ref.shape[1]):
        o_ref[0, r] = total[:, r * wide : (r + 1) * wide]


def finish(pairs, weights, height, wide):
    rows = 8
    _, _, snaps = pairs[0][0].shape
    share = weights.shape[0] // 2
    part = pl.BlockSpec((1, rows * wide, snaps), lambda k, i: (k, i, 0))
    return pl.pallas_call(
        finish_kernel,
        grid=(2, height // rows),
        in_specs=[part] * (2 * len(pairs))
        + [pl.BlockSpec(weights.shape, lambda k, i: (0, 0))],
        out_specs=pl.BlockSpec((1, rows, share, wide), lambda k, i: (k, i, 0, 0)),
        out_shape=jax.ShapeDtypeStruct((2, height, share, wide), F32),
        compiler_params=pltpu.CompilerParams(vmem_limit_bytes=LIMIT),
    )(*[array for pair in pairs for array in pair], weights)


def edges(block, axis, dim):
    count = lax.axis_size(axis)
    forward = [(i, i + 1) for i in range(count - 1)]
    backward = [(target, source) for source, target in forward]
    low = lax.ppermute(
        lax.slice_in_dim(block, block.shape[dim] - 1, None, axis=dim), axis, forward
    )
    high = lax.ppermute(lax.slice_in_dim(block, 0, 1, axis=dim), axis, backward)
    return low, high


def halo_of(block):
    x_low, x_high = edges(block, "gx", 1)
    y_low, y_high = edges(block, "gy", 2)
    low = jnp.concatenate([x_low[:, 0], y_low[:, :, 0]], axis=1)
    high = jnp.concatenate([x_high[:, 0], y_high[:, :, 0]], axis=1)
    return jnp.stack([low, high], axis=1)


def swapped(value, mask):
    pairs = [(source, source ^ mask) for source in range(lax.axis_size("cyc"))]
    return lax.ppermute(value, "cyc", pairs)


def scatter_sum(value, axis):
    count = lax.axis_size(axis)
    parts = lax.all_to_all(value, axis, 0, 0, tiled=True)
    return parts.reshape(count, -1, value.shape[1]).sum(0)


def gathered(value, axis):
    count = lax.axis_size(axis)
    copies = jnp.broadcast_to(value[None], (count,) + value.shape)
    return lax.all_to_all(copies.reshape(-1, value.shape[1]), axis, 0, 0, tiled=True)


def all_sum(value):
    flat = value.reshape(-1, 128)
    part = scatter_sum(flat, "gx")
    part = gathered(part, "gy")
    part = part.reshape(lax.axis_size("gy"), -1, 128).sum(0)
    return gathered(part, "gx").reshape(value.shape)


def whole(displacement):
    _, height, wide, _ = displacement.shape
    groups = lax.axis_size("cyc")
    halo = halo_of(displacement)
    near = swapped(displacement, 1)
    side = swapped(displacement, 3)
    near_halo, far_halo, side_halo = (swapped(halo, mask) for mask in (1, 2, 3))
    own, gram = features(displacement, halo, [])
    total = all_sum(gram)
    level0 = first_level(total)
    other0 = swapped(level0, 1)
    relayed, _ = lax.optimization_barrier((near, total))
    far = swapped(relayed, 3)
    pair, cross1 = features(near, near_halo, [own])
    total = all_sum(project(level0, other0, [cross1]))
    level1 = next_level(level0, total, other0)
    other1 = swapped(level1, 2)
    fourth, cross3 = features(side, side_halo, [own, pair])
    third, cross2 = features(far, far_halo, [own, pair])
    share = RANK // groups
    column = lax.axis_index("cyc") * share + jnp.arange(share)
    pick = (column[:, None] == jnp.arange(RANK)[None, :]).astype(F32)
    total = all_sum(project(level1, other1, [cross2, cross3]))
    weights = last_level(level1, total, other1, pick)
    result = finish([own, pair, third, fourth], weights, height, wide)
    return result.transpose(0, 1, 3, 2)


def solution(mesh):
    return jax.shard_map(
        whole,
        mesh=mesh,
        in_specs=(P(None, "gx", "gy", "cyc"),),
        out_specs=P(None, "gx", "gy", "cyc"),
        check_vma=False,
    )
```
